32 devices in a mesh: seq: 8 (over z, y), tp: 4 (over x, core).
Axes of the slice: x: 2, y: 2, z: 4, core: 2. Of those that a mesh axis runs over, the one named last changes fastest.
Arguments:
- attention_output: bfloat16 [6144, 4096], P('seq', 'tp'), may hold values from -6 to 6
- output_gradient: bfloat16 [6144, 4096], P('seq', 'tp'), may hold values from -6 to 6
- output_weight: bfloat16 [4096, 4096], P('tp'), may hold values from -0.09375 to 0.09375
- adapter_down: bfloat16 [32, 64, 4096], P('seq', None, 'tp'), may hold values from -0.09375 to 0.09375
- adapter_up: bfloat16 [32, 64, 4096], P('seq', None, 'tp'), may hold values from -0.75 to 0.75
- momentum_down: float32 [32, 64, 4096], P('seq', None, 'tp'), may hold values from -6 to 6
- momentum_up: float32 [32, 64, 4096], P('seq', None, 'tp'), may hold values from -6 to 6
- tenant_storage_row: int32 [32], replicated, may hold values from 0 to 31, as said below
- slot_tenant_index: int32 [8, 4], replicated, may hold values from 0 to 31, as said below
- slot_token_rows: int32 [8, 4], replicated, may hold values from 1 to 288, 768 in all within a row
Outputs:
- out_act: bfloat16 [6144, 4096], P('seq', 'tp')
- in_grad: bfloat16 [6144, 4096], P('seq', 'tp')
- step_down: float32 [32, 64, 4096], P('seq', None, 'tp')
- step_up: float32 [32, 64, 4096], P('seq', None, 'tp')
- new_moment_down: float32 [32, 64, 4096], P('seq', None, 'tp')
- new_moment_up: float32 [32, 64, 4096], P('seq', None, 'tp')
The draws below stay inside these ranges and needn't reach their ends.
Inputs may be any that keep to these rules, and one draw needn't show every extreme that they name: A permutation: tenant t's adapters and momenta are row tenant_storage_row[t], owned by seq index tenant_storage_row[t] // 4. `slot_tenant_index`: the 4 tenants of one seq index have distinct owners; a tenant may stand on several seq indices or on none. `slot_token_rows`: each row sums to 768.
All inputs are finite; a program needn't handle non-finite values.
Results may differ from the reference program's by a relative error of at most 0.014.
Values may be sent and summed in bfloat16 or wider, within the bound.
A program may use at most 128 MiB of HBM per device.

```python
import math
import jax
import jax.numpy as jnp
import numpy as np
from jax import lax

FEATURES_INPUT = 4096
FEATURES_OUTPUT = 4096
ADAPTER_RANK = 64
TOKEN_ROWS_LOCAL = 768
SLOTS_PER_SEQ = 4
TEN_DEV = 4
TENANT_TOTAL = 32
TOKENS = 6144
MOST = 288
N_SEQ = 8
N_TP = 4


def layout_tables(key):
    folded = jax.random.fold_in(key, 11)
    keys = jax.random.split(folded, 3)
    storage = jax.random.permutation(keys[0], TENANT_TOTAL).astype(jnp.int32)
    inverse = jnp.zeros((TENANT_TOTAL,), jnp.int32).at[storage].set(jnp.arange(TENANT_TOTAL, dtype=jnp.int32))
    row_keys = jax.random.split(keys[1], N_SEQ)
    owners = jax.vmap(lambda single: jax.random.permutation(single, N_SEQ))(row_keys)[:, :SLOTS_PER_SEQ].astype(jnp.int32)
    within = jax.random.randint(keys[2], (N_SEQ, SLOTS_PER_SEQ), 0, TEN_DEV).astype(jnp.int32)
    tenants = inverse[owners * TEN_DEV + within]
    return (storage, tenants.astype(jnp.int32))


def draw_tenant_storage_row(key, part):
    return layout_tables(key)[0]


def draw_slot_tenant_index(key, part):
    return layout_tables(key)[1]


def steps_of(own_key, dims, cuts, low, top_value):
    def one(axis_at, shards_of):
        steps = jax.random.uniform(jax.random.fold_in(jax.random.fold_in(own_key, 6), axis_at), (shards_of,), jnp.float32, low / len(cuts), top_value / len(cuts))
        return jnp.repeat(jnp.exp(steps), dims[axis_at] // shards_of).reshape((-1,) + (1,) * (len(dims) - axis_at - 1))

    loudness = one(*cuts[0])
    for cut in cuts[1:]:
        loudness = loudness * one(*cut)
    return loudness


def profile(amount, total, most, lean):
    loads = [(1 << 20) // math.isqrt(standing ** lean) + 1 for standing in range(2, amount + 1)]
    surplus, holding = total - most - (amount - 1), [1] * (amount - 1)
    while surplus > 0:
        candidates = [i for i in range(amount - 1) if holding[i] < most]
        mass, left = sum([loads[i] for i in candidates]), surplus
        for i in candidates:
            extra = min(most - holding[i], max(1, left * loads[i] // mass), surplus)
            holding[i] = holding[i] + extra
            surplus = surplus - extra
    return np.array([most] + holding)


def uneven(rng, number_of, total, bound, skew):
    if number_of == 2:
        one = jax.random.randint(rng, (), max(1, total - bound), min(bound, total - 1) + 1)
        return jnp.stack([one, total - one])
    lengths = jnp.asarray(profile(number_of, total, bound, skew), jnp.int32)
    twos = (number_of - 1) // 2
    donor, receiver = lengths[1:1 + 2 * twos:2], lengths[2:2 + 2 * twos:2]
    slack = jnp.minimum(donor - 1, bound - receiver)
    moved = jax.random.randint(jax.random.fold_in(rng, 1), (twos,), 0, 1 << 20) % (slack + 1)
    lengths = lengths.at[1:1 + 2 * twos:2].set(donor - moved).at[2:2 + 2 * twos:2].set(receiver + moved)
    return lengths[jax.random.permutation(jax.random.fold_in(rng, 2), number_of)]


def centred(stream_key, dims, scale, bound, cuts=(), held_as=jnp.bfloat16):
    result = jax.random.normal(stream_key, dims, jnp.float32) * scale
    if len(cuts) > 0:
        result = steps_of(stream_key, dims, cuts, -0.22, 0.18) * result
    return jnp.clip(result, min=-bound, max=bound).astype(held_as)


def setup_inputs(seed: int = 0) -> dict:
    arg_keys = jax.random.split(jax.random.key(seed), 11)
    attention_output = centred(arg_keys[0], (TOKENS, FEATURES_INPUT), 1.0, 6.0, ((0, 8), (1, 4)))
    output_gradient = centred(arg_keys[1], (TOKENS, FEATURES_OUTPUT), 1.0, 6.0, ((0, 8), (1, 4)))
    output_weight = centred(arg_keys[2], (FEATURES_INPUT, FEATURES_OUTPUT), FEATURES_INPUT ** -0.5, 0.09375, ((0, 4),))
    adapter_down = centred(arg_keys[3], (TENANT_TOTAL, ADAPTER_RANK, FEATURES_INPUT), FEATURES_INPUT ** -0.5, 0.09375, ((0, 8), (2, 4)))
    adapter_up = centred(arg_keys[4], (TENANT_TOTAL, ADAPTER_RANK, FEATURES_OUTPUT), ADAPTER_RANK ** -0.5, 0.75, ((0, 8), (2, 4)))
    momentum_down = centred(arg_keys[5], (TENANT_TOTAL, ADAPTER_RANK, FEATURES_INPUT), 1.0, 6.0, ((0, 8), (2, 4)), jnp.float32)
    momentum_up = centred(arg_keys[6], (TENANT_TOTAL, ADAPTER_RANK, FEATURES_OUTPUT), 1.0, 6.0, ((0, 8), (2, 4)), jnp.float32)
    tenant_storage_row = draw_tenant_storage_row(jax.random.fold_in(arg_keys[10], 71), 0)
    slot_tenant_index = draw_slot_tenant_index(jax.random.fold_in(arg_keys[10], 71), 0)
    slot_token_rows = jax.vmap(lambda own: uneven(own, SLOTS_PER_SEQ, TOKEN_ROWS_LOCAL, MOST, 2))(jax.random.split(arg_keys[9], N_SEQ)).reshape((N_SEQ, SLOTS_PER_SEQ)).astype(jnp.int32)
    return dict(attention_output=attention_output, output_gradient=output_gradient, output_weight=output_weight, adapter_down=adapter_down, adapter_up=adapter_up, momentum_down=momentum_down, momentum_up=momentum_up, tenant_storage_row=tenant_storage_row, slot_tenant_index=slot_tenant_index, slot_token_rows=slot_token_rows)


adapter_scale = 2.0
beta_first = 0.9
beta_second = 0.99
soft_floor = 0.25
epsilon = 1e-06

def slot_positions(tenant_storage_row, slot_tenant_index):
    tenant_ids = jnp.arange(tenant_storage_row.shape[0], dtype=jnp.int32)
    match = slot_tenant_index[:, :, None] == tenant_ids[None, None, :]
    return lax.optimization_barrier(jnp.sum(jnp.where(match, tenant_storage_row[None, None, :], 0), axis=2)).astype(jnp.int32)

def row_members(counts, row_count):
    ends = jnp.cumsum(counts)
    starts = ends - counts
    index = jnp.arange(row_count, dtype=jnp.int32)
    return (index[:, None] >= starts[None, :]) & (index[:, None] < ends[None, :])

def lion_step(moment, grad):
    combined = beta_first * moment + (1.0 - beta_first) * grad
    spread = jnp.sqrt(lax.optimization_barrier(jnp.mean(combined * combined, axis=1, keepdims=True)) + epsilon)
    step = combined / (jnp.abs(combined) + soft_floor * spread)
    return (step, beta_second * moment + (1.0 - beta_second) * grad)

def reference(attention_output, output_gradient, output_weight, adapter_down, adapter_up, momentum_down, momentum_up, tenant_storage_row, slot_tenant_index, slot_token_rows):
    slot_location = slot_positions(tenant_storage_row, slot_tenant_index)
    block_in = FEATURES_INPUT // N_TP
    contract_last = (((1,), (1,)), ((), ()))
    contract_leading = (((0,), (0,)), ((), ()))

    def one_device(items):
        inputs, given_gradients, down_tiles_list, up_tiles_list, counts = items
        tenant_mask = row_members(counts, TOKEN_ROWS_LOCAL)[:, :, None]
        flat_down = down_tiles_list.reshape(SLOTS_PER_SEQ * ADAPTER_RANK, FEATURES_INPUT)
        flattened_up = up_tiles_list.reshape(SLOTS_PER_SEQ * ADAPTER_RANK, FEATURES_OUTPUT)
        project = lax.dot_general(inputs, flat_down, contract_last, preferred_element_type=jnp.float32)
        low = lax.optimization_barrier(jnp.sum(jnp.where(tenant_mask, project.reshape(TOKEN_ROWS_LOCAL, SLOTS_PER_SEQ, ADAPTER_RANK), 0.0), axis=1)).astype(jnp.bfloat16)
        backward_pass = lax.dot_general(given_gradients, flattened_up, contract_last, preferred_element_type=jnp.float32)
        lowrank_gradient = (adapter_scale * lax.optimization_barrier(jnp.sum(jnp.where(tenant_mask, backward_pass.reshape(TOKEN_ROWS_LOCAL, SLOTS_PER_SEQ, ADAPTER_RANK), 0.0), axis=1))).astype(jnp.bfloat16)
        spread_lowrank = jnp.where(tenant_mask, low[:, None, :], jnp.zeros((), jnp.bfloat16)).reshape(TOKEN_ROWS_LOCAL, SLOTS_PER_SEQ * ADAPTER_RANK)
        spread_grad = jnp.where(tenant_mask, lowrank_gradient[:, None, :], jnp.zeros((), jnp.bfloat16)).reshape(TOKEN_ROWS_LOCAL, SLOTS_PER_SEQ * ADAPTER_RANK)
        base_output = jnp.zeros((TOKEN_ROWS_LOCAL, FEATURES_OUTPUT), jnp.float32)
        for block in range(N_TP):
            partial_out = jnp.dot(inputs[:, block * block_in:(block + 1) * block_in], output_weight[block * block_in:(block + 1) * block_in], preferred_element_type=jnp.float32)
            rounded = lax.optimization_barrier(partial_out.astype(jnp.bfloat16))
            base_output = base_output + rounded.astype(jnp.float32)
        output_rows = (base_output + adapter_scale * jnp.dot(spread_lowrank, flattened_up, preferred_element_type=jnp.float32)).astype(jnp.bfloat16)
        back_base = lax.dot_general(given_gradients, output_weight, contract_last, preferred_element_type=jnp.float32)
        in_rows = (back_base + jnp.dot(spread_grad, flat_down, preferred_element_type=jnp.float32)).astype(jnp.bfloat16)
        part_down = lax.dot_general(spread_grad, inputs, contract_leading, preferred_element_type=jnp.float32).astype(jnp.bfloat16)
        partial_up = (adapter_scale * lax.dot_general(spread_lowrank, given_gradients, contract_leading, preferred_element_type=jnp.float32)).astype(jnp.bfloat16)
        return (output_rows, in_rows, part_down.reshape(SLOTS_PER_SEQ, ADAPTER_RANK, FEATURES_INPUT), partial_up.reshape(SLOTS_PER_SEQ, ADAPTER_RANK, FEATURES_OUTPUT))
    down_tiles_list = adapter_down[slot_location]
    up_tiles_list = adapter_up[slot_location]
    results = lax.map(one_device, (attention_output.reshape(N_SEQ, TOKEN_ROWS_LOCAL, FEATURES_INPUT), output_gradient.reshape(N_SEQ, TOKEN_ROWS_LOCAL, FEATURES_OUTPUT), down_tiles_list, up_tiles_list, slot_token_rows))
    out_act = results[0].reshape(N_SEQ * TOKEN_ROWS_LOCAL, FEATURES_OUTPUT)
    in_grad = results[1].reshape(N_SEQ * TOKEN_ROWS_LOCAL, FEATURES_INPUT)
    flat_position = slot_location.reshape(-1)
    total_down = jnp.zeros((TENANT_TOTAL, ADAPTER_RANK, FEATURES_INPUT), jnp.float32).at[flat_position].add(results[2].reshape(N_SEQ * SLOTS_PER_SEQ, ADAPTER_RANK, FEATURES_INPUT).astype(jnp.float32))
    total_up = jnp.zeros((TENANT_TOTAL, ADAPTER_RANK, FEATURES_OUTPUT), jnp.float32).at[flat_position].add(results[3].reshape(N_SEQ * SLOTS_PER_SEQ, ADAPTER_RANK, FEATURES_OUTPUT).astype(jnp.float32))
    tokens = jnp.zeros((TENANT_TOTAL,), jnp.int32).at[flat_position].add(slot_token_rows.reshape(-1).astype(jnp.int32))
    denom = jnp.maximum(tokens, 1).astype(jnp.float32)
    step_down, new_moment_down = lion_step(momentum_down, total_down / denom[:, None, None])
    step_up, new_moment_up = lion_step(momentum_up, total_up / denom[:, None, None])
    return (out_act, in_grad, step_down, step_up, new_moment_down, new_moment_up)
```

```python
import functools

import jax
import jax.numpy as jnp
from jax import lax
from jax.experimental import pallas as pl
from jax.experimental.pallas import tpu as pltpu
from jax.sharding import PartitionSpec as P

adapter_scale = 2.0
beta_first = 0.9
beta_second = 0.99
soft_floor = 0.25
epsilon = 1e-06
contract_last = (((1,), (1,)), ((), ()))
contract_leading = (((0,), (0,)), ((), ()))
MESH = pl.DeviceIdType.MESH
cores = 2


def matmul(a, b, dims=(((1,), (0,)), ((), ()))):
    return lax.dot_general(a, b, dims, preferred_element_type=jnp.float32)


def step_kernel(
    seq_count, tp_count, chunks,
    storage_ref, tenant_ref, count_ref, x_hbm, g_hbm, w_hbm, down_hbm, up_hbm,
    out_hbm, in_hbm, inc_down, inc_up,
    x_v, w_v, gath, down_v, up_v, send_down, send_up, recv_down, recv_up, slot_down, slot_up,
    part, psend_down, psend_up, mine, psib, srecv, acc, in_v, packed, half_recv, half_sum, sum_recv, low_all,
    local_sem, ag_send, ag_recv, a2a_send, a2a_recv, sib_send, sib_recv, sx_send, sx_recv, rank_send, rank_recv, own_sem,
):
    s = lax.axis_index("seq")
    t = lax.axis_index("tp")
    chips = tp_count // cores
    chip = t // cores
    core = t % cores
    row_count, width = x_v.shape
    owned, rank, _ = down_v.shape
    slots = slot_down.shape[0] // rank
    sib = {"tp": chip * cores + 1 - core}
    half = row_count // 2
    quarter = half // 2
    step = row_count // chunks
    tile = min(256, width)
    pair = 2 * rank

    def tp_of(d, c):
        return lax.rem(chip + d, chips) * cores + c

    def rem_seq(k):
        return lax.rem(s + k, seq_count)

    loads = [
        pltpu.make_async_copy(up_hbm, up_v, local_sem.at[0]),
        pltpu.make_async_copy(down_hbm, down_v, local_sem.at[1]),
        pltpu.make_async_copy(x_hbm, x_v, local_sem.at[2]),
        pltpu.make_async_copy(g_hbm, gath.at[t], local_sem.at[3]),
    ]
    for cp in loads:
        cp.start()
    quarters = []
    for d in list(range(1, chips)) + [0]:
        quarters += [(d, 0), (d, 1)]

    def q_index(d, same):
        return tp_of(d, core if same else 1 - core)

    w_loads = []
    for n, (d, same) in enumerate(quarters):
        q = q_index(d, same)
        cp = pltpu.make_async_copy(
            w_hbm.at[:, pl.ds(pl.multiple_of(q * width, width), width)], w_v.at[q], local_sem.at[4 + n]
        )
        cp.start()
        w_loads.append(cp)

    barrier = pltpu.get_barrier_semaphore()
    for k in range(1, seq_count):
        pl.semaphore_signal(barrier, inc=1, device_id={"seq": rem_seq(k)}, device_id_type=MESH)
    for d in range(1, chips):
        pl.semaphore_signal(barrier, inc=1, device_id={"tp": tp_of(d, core)}, device_id_type=MESH)
    pl.semaphore_signal(barrier, inc=1, device_id=sib, device_id_type=MESH)
    pl.semaphore_wait(barrier, seq_count - 1 + chips)

    def rows_of(c):
        return pl.ds(c * step, step)

    def ag(kind, d, c):
        if kind == "sib":
            src, slot, index, to = g_hbm.at[rows_of(c)], t, 0, sib
        elif kind == "chip":
            src, slot, index, to = g_hbm.at[rows_of(c)], t, d, {"tp": tp_of(d, core)}
        else:
            slot = tp_of(chips - d, core)
            src, index, to = gath.at[slot, rows_of(c)], chips - 1 + d, sib
        return pltpu.make_async_remote_copy(
            src_ref=src, dst_ref=gath.at[slot, rows_of(c)], send_sem=ag_send.at[index, c],
            recv_sem=ag_recv.at[index, c], device_id=to, device_id_type=MESH,
        )

    for c in range(chunks):
        for d in range(1, chips):
            ag("chip", d, c).start()
        ag("sib", 0, c).start()

    def forward(c):
        for d in range(1, chips):
            ag("chip", d, c).wait_recv()
            ag("pass", d, c).start()

    def place(i, j):
        return storage_ref[tenant_ref[i, j]]

    def picked(i):
        row = jnp.int32(0)
        for j in range(slots):
            p = place(i, j)
            row = row + jnp.where(p // owned == s, p % owned, 0)
        return row

    def slot_at(owner):
        found = jnp.int32(slots)
        for j in range(slots):
            found = jnp.where(place(s, j) // owned == owner, j, found)
        return found

    def bounds():
        pairs, at = [], jnp.int32(0)
        for j in range(slots):
            pairs.append((at, at + count_ref[s, j]))
            at = at + count_ref[s, j]
        return pairs

    spans = bounds()

    def a2a(n, k, src, dst):
        return pltpu.make_async_remote_copy(
            src_ref=src.at[rem_seq(k)], dst_ref=dst.at[s], send_sem=a2a_send.at[n, k],
            recv_sem=a2a_recv.at[n, k], device_id={"seq": rem_seq(k)}, device_id_type=MESH,
        )

    exchanges = [(send_up, recv_up), (send_down, recv_down), (psend_down, inc_down), (psend_up, inc_up)]

    def pick_send(n, table, send, recv):
        for k in range(1, seq_count):
            j = rem_seq(k)
            send[j] = table[picked(j)]
            a2a(n, k, send, recv).start()
        recv[s] = table[picked(s)]

    loads[0].wait()
    pick_send(0, up_v, send_up, recv_up)
    loads[1].wait()
    pick_send(1, down_v, send_down, recv_down)

    def sib_copy(d):
        q = q_index(d, 0)
        return pltpu.make_async_remote_copy(
            src_ref=mine.at[q], dst_ref=psib.at[lax.rem(chip + d, chips)], send_sem=sib_send.at[d],
            recv_sem=sib_recv.at[d], device_id=sib, device_id_type=MESH,
        )

    loads[2].wait()
    for n, (d, same) in enumerate(quarters):
        q = q_index(d, same)
        w_loads[n].wait()

        @pl.loop(0, width // tile)
        def _(j):
            cols = pl.ds(pl.multiple_of(j * tile, tile), tile)
            mine[q, :, cols] = matmul(x_v[...], w_v[q, :, cols]).astype(jnp.bfloat16)

        if not same:
            sib_copy(d).start()

    def back_term(slot, first=False):
        @pl.loop(0, width // tile)
        def _(j):
            cols = pl.ds(pl.multiple_of(j * tile, tile), tile)
            term = matmul(gath[slot], w_v[slot, cols, :], contract_last)
            if first:
                acc[:, cols] = term
            else:
                acc[:, cols] = acc[:, cols] + term

    loads[3].wait()
    back_term(t, True)
    forward(0)
    for c in range(chunks):
        ag("sib", 0, c).wait_recv()
    back_term(sib["tp"])
    forward(1)

    def sx(d, c):
        return pltpu.make_async_remote_copy(
            src_ref=mine.at[tp_of(d, core), rows_of(c)], dst_ref=srecv.at[chip, rows_of(c)], send_sem=sx_send.at[d, c],
            recv_sem=sx_recv.at[d, c], device_id={"tp": tp_of(d, core)}, device_id_type=MESH,
        )

    for d in range(1, chips):
        q = tp_of(d, core)
        sib_copy(d).wait_recv()
        for c in range(chunks):
            @pl.loop(0, step // 64)
            def _(j):
                rows = pl.ds(pl.multiple_of(c * step + j * 64, 64), 64)
                both = mine[q, rows, :].astype(jnp.float32) + psib[lax.rem(chip + d, chips), rows, :].astype(jnp.float32)
                mine[q, rows, :] = both.astype(jnp.bfloat16)

            sx(d, c).start()

    block = 64 if half % 64 == 0 else 16
    lane = lax.broadcasted_iota(jnp.int32, (block, pair), 1)
    row_iota = lax.broadcasted_iota(jnp.int32, (block, pair), 0)

    def member(group, first_row):
        lo = jnp.where(lane < rank, spans[2 * group][0], spans[2 * group + 1][0]) - first_row
        hi = jnp.where(lane < rank, spans[2 * group][1], spans[2 * group + 1][1]) - first_row
        return (row_iota >= lo) & (row_iota < hi)

    def gather_slots(recv, slot_v):
        for j in range(slots):
            slot_v[j * rank:(j + 1) * rank] = recv[place(s, j) // owned]

    def project(n, rows_at, slot_v):
        @pl.loop(0, half // block)
        def _(j):
            both = []
            for side in range(2):
                first_row = j * block + side * half
                product = matmul(rows_at(first_row), slot_v[...], contract_last)
                total = jnp.zeros((block, pair), jnp.float32)
                for group in range(slots // 2):
                    total = total + jnp.where(member(group, first_row), product[:, group * pair:(group + 1) * pair], 0.0)
                both.append(total + pltpu.roll(total, rank, 1))
            packed[n, pl.ds(pl.multiple_of(j * block, block), block)] = jnp.where(lane < rank, both[0], both[1]).astype(jnp.bfloat16)

    def rank_copy(n, kind, d=0):
        if kind == "half":
            src, dst, index, to = packed.at[n, pl.ds(pl.multiple_of((1 - core) * quarter, quarter), quarter)], half_recv.at[n], 0, sib
        elif kind == "chip":
            src, dst, index, to = half_sum.at[n], sum_recv.at[n, chip], d, {"tp": tp_of(d, core)}
        else:
            at = pl.ds(pl.multiple_of(core * quarter, quarter), quarter)
            src, dst, index, to = low_all.at[n, at], low_all.at[n, at], chips, sib
        return pltpu.make_async_remote_copy(
            src_ref=src, dst_ref=dst, send_sem=rank_send.at[n, index], recv_sem=rank_recv.at[n, index],
            device_id=to, device_id_type=MESH,
        )

    def reduce_first(n):
        rank_copy(n, "half").start()
        rank_copy(n, "half").wait_recv()
        own = packed[n, pl.ds(pl.multiple_of(core * quarter, quarter), quarter)].astype(jnp.float32)
        half_sum[n] = (own + half_recv[n].astype(jnp.float32)).astype(jnp.bfloat16)
        for d in range(1, chips):
            rank_copy(n, "chip", d).start()

    def reduce_last(n, scale):
        total = half_sum[n].astype(jnp.float32)
        for d in range(1, chips):
            rank_copy(n, "chip", d).wait_recv()
            total = total + sum_recv[n, lax.rem(chip + chips - d, chips)].astype(jnp.float32)
        low_all[n, pl.ds(pl.multiple_of(core * quarter, quarter), quarter)] = (scale * total).astype(jnp.bfloat16)
        rank_copy(n, "whole").start()
        rank_copy(n, "whole").wait_recv()

    def spread(n, j, side):
        values = low_all[n, pl.ds(pl.multiple_of(j * block, block), block)].astype(jnp.float32)
        turned = pltpu.roll(values, rank, 1)
        wide = jnp.where((lane < rank) == (side == 0), values, turned)
        first_row = j * block + side * half
        return jnp.concatenate(
            [jnp.where(member(group, first_row), wide, 0.0).astype(jnp.bfloat16) for group in range(slots // 2)], axis=1
        )

    def spread_into(n, wide_v):
        for side in range(2):
            @pl.loop(0, half // block)
            def _(j):
                wide_v[pl.ds(pl.multiple_of(side * half + j * block, block), block)] = spread(n, j, side)

    part[slots] = jnp.zeros((rank, width), jnp.bfloat16)

    def return_parts(n, wide_v, rows, scale, psend, incoming):
        @pl.loop(0, width // tile)
        def _(j):
            cols = pl.ds(pl.multiple_of(j * tile, tile), tile)
            term = (scale * matmul(wide_v[...], rows[:, cols], contract_leading)).astype(jnp.bfloat16)
            for k in range(slots):
                part[k, :, cols] = term[k * rank:(k + 1) * rank]

        for k in range(1, seq_count):
            j = rem_seq(k)
            psend[j] = part[slot_at(j)]
            a2a(n, k, psend, incoming).start()
        psend[s] = part[slot_at(s)]
        pltpu.make_async_copy(psend.at[s], incoming.at[s], own_sem.at[n - 2]).start()

    def run(wide_grad, wide_low):
        for k in range(1, seq_count):
            a2a(0, k, send_up, recv_up).wait_recv()
        gather_slots(recv_up, slot_up)
        project(0, lambda at: gath[t, pl.ds(pl.multiple_of(at, block), block)], slot_up)
        reduce_first(0)
        for c in range(2, chunks):
            forward(c)
        reduce_last(0, adapter_scale)
        spread_into(0, wide_grad)
        return_parts(2, wide_grad, x_v, 1.0, psend_down, inc_down)

        for k in range(1, seq_count):
            a2a(1, k, send_down, recv_down).wait_recv()
        gather_slots(recv_down, slot_down)
        project(1, lambda at: x_v[pl.ds(pl.multiple_of(at, block), block)], slot_down)
        reduce_first(1)
        for d in range(1, chips):
            back_term(tp_of(chips - d, core))
        reduce_last(1, 1.0)
        spread_into(1, wide_low)
        return_parts(3, wide_low, gath.at[t], adapter_scale, psend_up, inc_up)

        for d in range(1, chips):
            for c in range(chunks):
                ag("pass", d, c).wait_recv()
            back_term(tp_of(chips - d, 1 - core))

        @pl.loop(0, width // tile)
        def _(j):
            cols = pl.ds(pl.multiple_of(j * tile, tile), tile)
            in_v[:, cols] = (acc[:, cols] + matmul(wide_grad[...], slot_down[:, cols])).astype(jnp.bfloat16)

        in_copy = pltpu.make_async_copy(in_v, in_hbm, own_sem.at[2])
        in_copy.start()

        sib_copy(0).wait_recv()

        @pl.loop(0, width // tile)
        def _(j):
            cols = pl.ds(pl.multiple_of(j * tile, tile), tile)
            base = mine[t, :, cols].astype(jnp.float32) + psib[chip, :, cols].astype(jnp.float32)
            acc[:, cols] = base + adapter_scale * matmul(wide_low[...], slot_up[:, cols])

        outs = []
        for c in range(chunks):
            for d in range(1, chips):
                sx(d, c).wait_recv()

            @pl.loop(0, step // 64)
            def _(j):
                rows = pl.ds(pl.multiple_of(c * step + j * 64, 64), 64)
                total = acc[rows, :]
                for d in range(1, chips):
                    total = total + srecv[lax.rem(chip + chips - d, chips), rows, :].astype(jnp.float32)
                mine[t, rows, :] = total.astype(jnp.bfloat16)

            cp = pltpu.make_async_copy(mine.at[t, rows_of(c)], out_hbm.at[rows_of(c)], own_sem.at[3 + c])
            cp.start()
            outs.append(cp)
        in_copy.wait()
        for cp in outs:
            cp.wait()

    pl.run_scoped(
        run,
        pltpu.VMEM((row_count, slots * rank), jnp.bfloat16),
        pltpu.VMEM((row_count, slots * rank), jnp.bfloat16),
    )

    for c in range(chunks):
        ag("sib", 0, c).wait_send()
        for d in range(1, chips):
            ag("chip", d, c).wait_send()
            ag("pass", d, c).wait_send()
            sx(d, c).wait_send()
    for d in range(chips):
        sib_copy(d).wait_send()
    for n in range(2):
        rank_copy(n, "half").wait_send()
        rank_copy(n, "whole").wait_send()
        for d in range(1, chips):
            rank_copy(n, "chip", d).wait_send()
    for n, (src, dst) in enumerate(exchanges):
        for k in range(1, seq_count):
            a2a(n, k, src, dst).wait_send()
    for n in (2, 3):
        src, dst = exchanges[n]
        pltpu.make_async_copy(src.at[s], dst.at[s], own_sem.at[n - 2]).wait()
        for k in range(1, seq_count):
            a2a(n, k, src, dst).wait_recv()


def adapter_step(storage, tenants, counts, x, g, w, down, up, seq_count, tp_count):
    row_count, width = x.shape
    owned, rank, _ = down.shape
    slots = tenants.shape[1]
    chips = tp_count // cores
    chunks = 3 if row_count % 3 == 0 else 2
    bf16, f32 = jnp.bfloat16, jnp.float32
    dma = pltpu.SemaphoreType.DMA
    smem = pl.BlockSpec(memory_space=pltpu.SMEM)
    hbm = pl.BlockSpec(memory_space=pl.ANY)
    blocks = (seq_count, rank, width)
    vmem = lambda shape, dtype=bf16: pltpu.VMEM(shape, dtype)
    half = row_count // 2
    return pl.pallas_call(
        functools.partial(step_kernel, seq_count, tp_count, chunks),
        out_shape=(
            jax.ShapeDtypeStruct((row_count, width), bf16),
            jax.ShapeDtypeStruct((row_count, width), bf16),
            jax.ShapeDtypeStruct(blocks, bf16),
            jax.ShapeDtypeStruct(blocks, bf16),
        ),
        in_specs=[smem] * 3 + [hbm] * 5,
        out_specs=(hbm,) * 4,
        scratch_shapes=[
            vmem((row_count, width)),
            vmem((tp_count, width, width)),
            vmem((tp_count, row_count, width)),
            vmem((owned, rank, width)),
            vmem((owned, rank, width)),
            vmem(blocks), vmem(blocks), vmem(blocks), vmem(blocks),
            vmem((slots * rank, width)),
            vmem((slots * rank, width)),
            vmem((slots + 1, rank, width)),
            vmem(blocks), vmem(blocks),
            vmem((tp_count, row_count, width)),
            vmem((chips, row_count, width)),
            vmem((chips, row_count, width)),
            vmem((row_count, width), f32),
            vmem((row_count, width)),
            vmem((2, half, 2 * rank)),
            vmem((2, half // 2, 2 * rank)),
            vmem((2, half // 2, 2 * rank)),
            vmem((2, chips, half // 2, 2 * rank)),
            vmem((2, half, 2 * rank)),
            dma((4 + tp_count,)),
            dma((2 * chips - 1, chunks)), dma((2 * chips - 1, chunks)),
            dma((4, seq_count)), dma((4, seq_count)),
            dma((chips,)), dma((chips,)),
            dma((chips, chunks)), dma((chips, chunks)),
            dma((2, chips + 1)), dma((2, chips + 1)),
            dma((3 + chunks,)),
        ],
        compiler_params=pltpu.CompilerParams(
            collective_id=0, has_side_effects=True, vmem_limit_bytes=60 * 1024 * 1024
        ),
        name="adapter_step",
    )(storage, tenants, counts, x, g, w, down, up)


def lion_kernel(storage_ref, tenant_ref, count_ref, inc_down, inc_up, mom_down, mom_up,
                step_down, step_up, new_down, new_up, total, row_at, used, tokens):
    seq_count, slots = tenant_ref.shape
    owned, rank, _ = mom_down.shape
    s = lax.axis_index("seq")

    @pl.when(pl.program_id(0) == 0)
    def _():
        for k in range(owned):
            tokens[k] = 0

        @pl.loop(0, seq_count)
        def _(i):
            row_at[i] = 0
            used[i] = 0
            for j in range(slots):
                p = storage_ref[tenant_ref[i, j]]
                here = (p // owned == s).astype(jnp.int32)
                k = p % owned
                row_at[i] = row_at[i] + here * k
                used[i] = used[i] + here
                tokens[k] = tokens[k] + here * count_ref[i, j]

    for incoming, moment_ref, step_ref, new_ref in (
        (inc_down, mom_down, step_down, new_down), (inc_up, mom_up, step_up, new_up)
    ):
        total[...] = jnp.zeros_like(total)

        @pl.loop(0, seq_count)
        def _(i):
            k = row_at[i]
            total[k] = total[k] + used[i].astype(jnp.float32) * incoming[i].astype(jnp.float32)

        for k in range(owned):
            grad = total[k] / jnp.maximum(tokens[k], 1).astype(jnp.float32)
            moment = moment_ref[k]
            combined = beta_first * moment + (1.0 - beta_first) * grad
            spread = jnp.sqrt(jnp.mean(combined * combined, axis=0, keepdims=True) + epsilon)
            step_ref[k] = combined / (jnp.abs(combined) + soft_floor * spread)
            new_ref[k] = beta_second * moment + (1.0 - beta_second) * grad


def lion(storage, tenants, counts, inc_down, inc_up, mom_down, mom_up):
    seq_count, rank, width = inc_down.shape
    owned = mom_down.shape[0]
    tile = min(256, width)
    block = pl.BlockSpec((owned, rank, tile), lambda j: (0, 0, j))
    many = pl.BlockSpec((seq_count, rank, tile), lambda j: (0, 0, j))
    shape = jax.ShapeDtypeStruct(mom_down.shape, jnp.float32)
    smem = pl.BlockSpec(memory_space=pltpu.SMEM)
    return pl.pallas_call(
        lion_kernel,
        out_shape=(shape,) * 4,
        grid=(width // tile,),
        in_specs=[smem] * 3 + [many, many, block, block],
        out_specs=(block,) * 4,
        scratch_shapes=[
            pltpu.VMEM((owned, rank, tile), jnp.float32),
            pltpu.SMEM((seq_count,), jnp.int32),
            pltpu.SMEM((seq_count,), jnp.int32),
            pltpu.SMEM((owned,), jnp.int32),
        ],
        compiler_params=pltpu.CompilerParams(vmem_limit_bytes=32 * 1024 * 1024),
        name="lion",
    )(storage, tenants, counts, inc_down, inc_up, mom_down, mom_up)


def local(seq_count, tp_count, x, g, w, down, up, mom_down, mom_up, storage, tenants, counts):
    out_act, in_grad, inc_down, inc_up = adapter_step(
        storage, tenants, counts, x, g, w, down, up, seq_count, tp_count
    )
    step_down, step_up, new_down, new_up = lion(storage, tenants, counts, inc_down, inc_up, mom_down, mom_up)
    return out_act, in_grad, step_down, step_up, new_down, new_up


def solution(mesh):
    owner = P("seq", None, "tp")
    return jax.shard_map(
        functools.partial(local, mesh.shape["seq"], mesh.shape["tp"]),
        mesh=mesh,
        in_specs=(P("seq", "tp"), P("seq", "tp"), P("tp", None), owner, owner, owner, owner, P(), P(), P()),
        out_specs=(P("seq", "tp"), P("seq", "tp"), owner, owner, owner, owner),
        check_vma=False,
    )
```

```python
import functools

import jax
import jax.numpy as jnp
from jax import lax
from jax.experimental import pallas as pl
from jax.experimental.pallas import tpu as pltpu
from jax.sharding import PartitionSpec as P

adapter_scale = 2.0
beta_first = 0.9
beta_second = 0.99
soft_floor = 0.25
epsilon = 1e-06
contract_last = (((1,), (1,)), ((), ()))
contract_leading = (((0,), (0,)), ((), ()))
MESH = pl.DeviceIdType.MESH
cores = 2


def matmul(a, b, dims=(((1,), (0,)), ((), ()))):
    return lax.dot_general(a, b, dims, preferred_element_type=jnp.float32)


def step_kernel(
    seq_count, tp_count, chunks,
    storage_ref, tenant_ref, count_ref, x_hbm, g_hbm, w_hbm, down_hbm, up_hbm,
    out_hbm, in_hbm, inc_down, inc_up,
    x_v, w_v, gath, down_v, up_v, send_down, send_up, recv_down, recv_up, slot_down, slot_up,
    part, psend_down, psend_up, mine, psib, srecv, acc, in_v, packed, half_recv, half_sum, sum_recv, low_all,
    local_sem, ag_send, ag_recv, a2a_send, a2a_recv, sib_send, sib_recv, sx_send, sx_recv, rank_send, rank_recv, own_sem,
):
    s = lax.axis_index("seq")
    t = lax.axis_index("tp")
    chips = tp_count // cores
    chip = t // cores
    core = t % cores
    row_count, width = x_v.shape
    owned, rank, _ = down_v.shape
    slots = slot_down.shape[0] // rank
    sib = {"tp": chip * cores + 1 - core}
    half = row_count // 2
    quarter = half // 2
    step = row_count // chunks
    tile = min(256, width)
    pair = 2 * rank
    part_rows = 64 if step % 64 == 0 else 16

    def tp_of(d, c):
        return lax.rem(chip + d, chips) * cores + c

    def rem_seq(k):
        return lax.rem(s + k, seq_count)

    loads = [
        pltpu.make_async_copy(up_hbm, up_v, local_sem.at[0]),
        pltpu.make_async_copy(down_hbm, down_v, local_sem.at[1]),
        pltpu.make_async_copy(x_hbm, x_v, local_sem.at[2]),
        pltpu.make_async_copy(g_hbm, gath.at[t], local_sem.at[3]),
    ]
    for cp in loads:
        cp.start()
    quarters = []
    for d in list(range(1, chips)) + [0]:
        quarters += [(d, 0), (d, 1)]

    def q_index(d, same):
        return tp_of(d, core if same else 1 - core)

    w_loads = []
    for n, (d, same) in enumerate(quarters):
        q = q_index(d, same)
        cp = pltpu.make_async_copy(
            w_hbm.at[:, pl.ds(pl.multiple_of(q * width, width), width)], w_v.at[q], local_sem.at[4 + n]
        )
        cp.start()
        w_loads.append(cp)

    barrier = pltpu.get_barrier_semaphore()
    for k in range(1, seq_count):
        pl.semaphore_signal(barrier, inc=1, device_id={"seq": rem_seq(k)}, device_id_type=MESH)
    for d in range(1, chips):
        pl.semaphore_signal(barrier, inc=1, device_id={"tp": tp_of(d, core)}, device_id_type=MESH)
    pl.semaphore_signal(barrier, inc=1, device_id=sib, device_id_type=MESH)
    pl.semaphore_wait(barrier, seq_count - 1 + chips)

    def rows_of(c):
        return pl.ds(c * step, step)

    def ag(kind, d, c):
        if kind == "sib":
            src, slot, index, to = g_hbm.at[rows_of(c)], t, 0, sib
        elif kind == "chip":
            src, slot, index, to = g_hbm.at[rows_of(c)], t, d, {"tp": tp_of(d, core)}
        else:
            slot = tp_of(chips - d, core)
            src, index, to = gath.at[slot, rows_of(c)], chips - 1 + d, sib
        return pltpu.make_async_remote_copy(
            src_ref=src, dst_ref=gath.at[slot, rows_of(c)], send_sem=ag_send.at[index, c],
            recv_sem=ag_recv.at[index, c], device_id=to, device_id_type=MESH,
        )

    for c in range(chunks):
        for d in range(1, chips):
            ag("chip", d, c).start()
        ag("sib", 0, c).start()

    def forward(c):
        for d in range(1, chips):
            ag("chip", d, c).wait_recv()
            ag("pass", d, c).start()

    def place(i, j):
        return storage_ref[tenant_ref[j, i]]

    def picked(i):
        row = jnp.int32(0)
        for j in range(slots):
            p = place(i, j)
            row = row + jnp.where(p // owned == s, p % owned, 0)
        return row

    def slot_at(owner):
        found = jnp.int32(slots)
        for j in range(slots):
            found = jnp.where(place(s, j) // owned == owner, j, found)
        return found

    def bounds():
        pairs, at = [], jnp.int32(0)
        for j in range(slots):
            pairs.append((at, at + count_ref[j, s]))
            at = at + count_ref[j, s]
        return pairs

    spans = bounds()

    def a2a(n, k, src, dst):
        return pltpu.make_async_remote_copy(
            src_ref=src.at[rem_seq(k)], dst_ref=dst.at[s], send_sem=a2a_send.at[n, k],
            recv_sem=a2a_recv.at[n, k], device_id={"seq": rem_seq(k)}, device_id_type=MESH,
        )

    exchanges = [(send_up, recv_up), (send_down, recv_down), (psend_down, inc_down), (psend_up, inc_up)]

    def pick_send(n, table, send, recv):
        for k in range(1, seq_count):
            j = rem_seq(k)
            send[j] = table[picked(j)]
            a2a(n, k, send, recv).start()
        recv[s] = table[picked(s)]

    loads[0].wait()
    pick_send(0, up_v, send_up, recv_up)
    loads[1].wait()
    pick_send(1, down_v, send_down, recv_down)

    def sib_copy(d):
        q = q_index(d, 0)
        return pltpu.make_async_remote_copy(
            src_ref=mine.at[q], dst_ref=psib.at[lax.rem(chip + d, chips)], send_sem=sib_send.at[d],
            recv_sem=sib_recv.at[d], device_id=sib, device_id_type=MESH,
        )

    loads[2].wait()
    for n, (d, same) in enumerate(quarters):
        q = q_index(d, same)
        w_loads[n].wait()

        @pl.loop(0, width // tile)
        def _(j):
            cols = pl.ds(pl.multiple_of(j * tile, tile), tile)
            mine[q, :, cols] = matmul(x_v[...], w_v[q, :, cols]).astype(jnp.bfloat16)

        if not same:
            sib_copy(d).start()

    def back_term(slot, first=False):
        @pl.loop(0, width // tile)
        def _(j):
            cols = pl.ds(pl.multiple_of(j * tile, tile), tile)
            term = matmul(gath[slot], w_v[slot, cols, :], contract_last)
            if first:
                acc[:, cols] = term
            else:
                acc[:, cols] = acc[:, cols] + term

    loads[3].wait()
    forward(0)
    back_term(t, True)
    early = max(1, chunks // 2)
    for c in range(1, early - 1):
        forward(c)
    for c in range(chunks):
        ag("sib", 0, c).wait_recv()
    back_term(sib["tp"])
    for c in range(max(1, early - 1), early):
        forward(c)

    def sx(d, c):
        return pltpu.make_async_remote_copy(
            src_ref=mine.at[tp_of(d, core), rows_of(c)], dst_ref=srecv.at[chip, rows_of(c)], send_sem=sx_send.at[d, c],
            recv_sem=sx_recv.at[d, c], device_id={"tp": tp_of(d, core)}, device_id_type=MESH,
        )

    for d in range(1, chips):
        q = tp_of(d, core)
        sib_copy(d).wait_recv()
        for c in range(chunks):
            @pl.loop(0, step // part_rows)
            def _(j):
                rows = pl.ds(pl.multiple_of(c * step + j * part_rows, part_rows), part_rows)
                both = mine[q, rows, :].astype(jnp.float32) + psib[lax.rem(chip + d, chips), rows, :].astype(jnp.float32)
                mine[q, rows, :] = both.astype(jnp.bfloat16)


    def send_sums(begin, end):
        for c in range(begin, end):
            for d in range(1, chips):
                sx(d, c).start()

    block = 64 if half % 64 == 0 else 16
    lane = lax.broadcasted_iota(jnp.int32, (block, pair), 1)
    row_iota = lax.broadcasted_iota(jnp.int32, (block, pair), 0)

    def member(group, first_row):
        lo = jnp.where(lane < rank, spans[2 * group][0], spans[2 * group + 1][0]) - first_row
        hi = jnp.where(lane < rank, spans[2 * group][1], spans[2 * group + 1][1]) - first_row
        return (row_iota >= lo) & (row_iota < hi)

    def gather_slots(recv, slot_v):
        for j in range(slots):
            slot_v[j * rank:(j + 1) * rank] = recv[place(s, j) // owned]

    def project(n, rows_at, slot_v):
        @pl.loop(0, half // block)
        def _(j):
            both = []
            for side in range(2):
                first_row = j * block + side * half
                product = matmul(rows_at(first_row), slot_v[...], contract_last)
                total = jnp.zeros((block, pair), jnp.float32)
                for group in range(slots // 2):
                    total = total + jnp.where(member(group, first_row), product[:, group * pair:(group + 1) * pair], 0.0)
                both.append(total + pltpu.roll(total, rank, 1))
            packed[n, pl.ds(pl.multiple_of(j * block, block), block)] = jnp.where(lane < rank, both[0], both[1]).astype(jnp.bfloat16)

    def rank_copy(n, kind, d=0):
        if kind == "half":
            src, dst, index, to = packed.at[n, pl.ds(pl.multiple_of((1 - core) * quarter, quarter), quarter)], half_recv.at[n], 0, sib
        elif kind == "chip":
            src, dst, index, to = half_sum.at[n], sum_recv.at[n, chip], d, {"tp": tp_of(d, core)}
        else:
            at = pl.ds(pl.multiple_of(core * quarter, quarter), quarter)
            src, dst, index, to = low_all.at[n, at], low_all.at[n, at], chips, sib
        return pltpu.make_async_remote_copy(
            src_ref=src, dst_ref=dst, send_sem=rank_send.at[n, index], recv_sem=rank_recv.at[n, index],
            device_id=to, device_id_type=MESH,
        )

    def reduce_first(n):
        rank_copy(n, "half").start()
        rank_copy(n, "half").wait_recv()
        own = packed[n, pl.ds(pl.multiple_of(core * quarter, quarter), quarter)].astype(jnp.float32)
        half_sum[n] = (own + half_recv[n].astype(jnp.float32)).astype(jnp.bfloat16)
        for d in range(1, chips):
            rank_copy(n, "chip", d).start()

    def reduce_last(n, scale):
        total = half_sum[n].astype(jnp.float32)
        for d in range(1, chips):
            rank_copy(n, "chip", d).wait_recv()
            total = total + sum_recv[n, lax.rem(chip + chips - d, chips)].astype(jnp.float32)
        low_all[n, pl.ds(pl.multiple_of(core * quarter, quarter), quarter)] = (scale * total).astype(jnp.bfloat16)
        rank_copy(n, "whole").start()
        rank_copy(n, "whole").wait_recv()

    def spread(n, j, side):
        values = low_all[n, pl.ds(pl.multiple_of(j * block, block), block)].astype(jnp.float32)
        turned = pltpu.roll(values, rank, 1)
        wide = jnp.where((lane < rank) == (side == 0), values, turned)
        first_row = j * block + side * half
        return jnp.concatenate(
            [jnp.where(member(group, first_row), wide, 0.0).astype(jnp.bfloat16) for group in range(slots // 2)], axis=1
        )

    def spread_into(n, wide_v):
        for side in range(2):
            @pl.loop(0, half // block)
            def _(j):
                wide_v[pl.ds(pl.multiple_of(side * half + j * block, block), block)] = spread(n, j, side)

    part[slots] = jnp.zeros((rank, width), jnp.bfloat16)

    def return_parts(n, wide_v, rows, scale, psend, incoming):
        @pl.loop(0, width // tile)
        def _(j):
            cols = pl.ds(pl.multiple_of(j * tile, tile), tile)
            term = (scale * matmul(wide_v[...], rows[:, cols], contract_leading)).astype(jnp.bfloat16)
            for k in range(slots):
                part[k, :, cols] = term[k * rank:(k + 1) * rank]

        for k in range(1, seq_count):
            j = rem_seq(k)
            psend[j] = part[slot_at(j)]
            a2a(n, k, psend, incoming).start()
        psend[s] = part[slot_at(s)]
        pltpu.make_async_copy(psend.at[s], incoming.at[s], own_sem.at[n - 2]).start()

    def run(wide_grad, wide_low):
        def finish_in():
            @pl.loop(0, width // tile)
            def _(j):
                cols = pl.ds(pl.multiple_of(j * tile, tile), tile)
                in_v[:, cols] = (acc[:, cols] + matmul(wide_grad[...], slot_down[:, cols])).astype(jnp.bfloat16)

            cp = pltpu.make_async_copy(in_v, in_hbm, own_sem.at[2])
            cp.start()
            return cp

        for k in range(1, seq_count):
            a2a(0, k, send_up, recv_up).wait_recv()
        gather_slots(recv_up, slot_up)
        project(0, lambda at: gath[t, pl.ds(pl.multiple_of(at, block), block)], slot_up)
        reduce_first(0)
        send_sums(0, min(2, chunks))
        for c in range(early, chunks):
            forward(c)
        reduce_last(0, adapter_scale)
        spread_into(0, wide_grad)
        return_parts(2, wide_grad, x_v, 1.0, psend_down, inc_down)

        for d in range(1, chips):
            back_term(tp_of(chips - d, core))
        for d in range(1, chips):
            for c in range(chunks):
                ag("pass", d, c).wait_recv()
            back_term(tp_of(chips - d, 1 - core))

        for k in range(1, seq_count):
            a2a(1, k, send_down, recv_down).wait_recv()
        gather_slots(recv_down, slot_down)
        project(1, lambda at: x_v[pl.ds(pl.multiple_of(at, block), block)], slot_down)
        reduce_first(1)
        send_sums(min(2, chunks), chunks)
        in_copy = finish_in()
        reduce_last(1, 1.0)
        spread_into(1, wide_low)
        return_parts(3, wide_low, gath.at[t], adapter_scale, psend_up, inc_up)

        sib_copy(0).wait_recv()

        @pl.loop(0, width // tile)
        def _(j):
            cols = pl.ds(pl.multiple_of(j * tile, tile), tile)
            base = mine[t, :, cols].astype(jnp.float32) + psib[chip, :, cols].astype(jnp.float32)
            acc[:, cols] = base + adapter_scale * matmul(wide_low[...], slot_up[:, cols])

        outs = []
        for c in range(chunks):
            for d in range(1, chips):
                sx(d, c).wait_recv()

            @pl.loop(0, step // part_rows)
            def _(j):
                rows = pl.ds(pl.multiple_of(c * step + j * part_rows, part_rows), part_rows)
                total = acc[rows, :]
                for d in range(1, chips):
                    total = total + srecv[lax.rem(chip + chips - d, chips), rows, :].astype(jnp.float32)
                mine[t, rows, :] = total.astype(jnp.bfloat16)

            cp = pltpu.make_async_copy(mine.at[t, rows_of(c)], out_hbm.at[rows_of(c)], own_sem.at[3 + c])
            cp.start()
            outs.append(cp)
        in_copy.wait()
        for cp in outs:
            cp.wait()

    pl.run_scoped(
        run,
        pltpu.VMEM((row_count, slots * rank), jnp.bfloat16),
        pltpu.VMEM((row_count, slots * rank), jnp.bfloat16),
    )

    for c in range(chunks):
        ag("sib", 0, c).wait_send()
        for d in range(1, chips):
            ag("chip", d, c).wait_send()
            ag("pass", d, c).wait_send()
            sx(d, c).wait_send()
    for d in range(chips):
        sib_copy(d).wait_send()
    for n in range(2):
        rank_copy(n, "half").wait_send()
        rank_copy(n, "whole").wait_send()
        for d in range(1, chips):
            rank_copy(n, "chip", d).wait_send()
    for n, (src, dst) in enumerate(exchanges):
        for k in range(1, seq_count):
            a2a(n, k, src, dst).wait_send()
    for n in (2, 3):
        src, dst = exchanges[n]
        pltpu.make_async_copy(src.at[s], dst.at[s], own_sem.at[n - 2]).wait()
        for k in range(1, seq_count):
            a2a(n, k, src, dst).wait_recv()


def adapter_step(storage, tenants, counts, x, g, w, down, up, seq_count, tp_count):
    row_count, width = x.shape
    owned, rank, _ = down.shape
    slots = tenants.shape[0]
    chips = tp_count // cores
    chunks = next(n for n in (6, 3, 2, 1) if row_count % (16 * n) == 0)
    bf16, f32 = jnp.bfloat16, jnp.float32
    dma = pltpu.SemaphoreType.DMA
    smem = pl.BlockSpec(memory_space=pltpu.SMEM)
    hbm = pl.BlockSpec(memory_space=pl.ANY)
    blocks = (seq_count, rank, width)
    vmem = lambda shape, dtype=bf16: pltpu.VMEM(shape, dtype)
    half = row_count // 2
    return pl.pallas_call(
        functools.partial(step_kernel, seq_count, tp_count, chunks),
        out_shape=(
            jax.ShapeDtypeStruct((row_count, width), bf16),
            jax.ShapeDtypeStruct((row_count, width), bf16),
            jax.ShapeDtypeStruct(blocks, bf16),
            jax.ShapeDtypeStruct(blocks, bf16),
        ),
        in_specs=[smem] * 3 + [hbm] * 5,
        out_specs=(hbm,) * 4,
        scratch_shapes=[
            vmem((row_count, width)),
            vmem((tp_count, width, width)),
            vmem((tp_count, row_count, width)),
            vmem((owned, rank, width)),
            vmem((owned, rank, width)),
            vmem(blocks), vmem(blocks), vmem(blocks), vmem(blocks),
            vmem((slots * rank, width)),
            vmem((slots * rank, width)),
            vmem((slots + 1, rank, width)),
            vmem(blocks), vmem(blocks),
            vmem((tp_count, row_count, width)),
            vmem((chips, row_count, width)),
            vmem((chips, row_count, width)),
            vmem((row_count, width), f32),
            vmem((row_count, width)),
            vmem((2, half, 2 * rank)),
            vmem((2, half // 2, 2 * rank)),
            vmem((2, half // 2, 2 * rank)),
            vmem((2, chips, half // 2, 2 * rank)),
            vmem((2, half, 2 * rank)),
            dma((4 + tp_count,)),
            dma((2 * chips - 1, chunks)), dma((2 * chips - 1, chunks)),
            dma((4, seq_count)), dma((4, seq_count)),
            dma((chips,)), dma((chips,)),
            dma((chips, chunks)), dma((chips, chunks)),
            dma((2, chips + 1)), dma((2, chips + 1)),
            dma((3 + chunks,)),
        ],
        compiler_params=pltpu.CompilerParams(
            collective_id=0, has_side_effects=True, vmem_limit_bytes=60 * 1024 * 1024
        ),
        name="adapter_step",
    )(storage, tenants, counts, x, g, w, down, up)


def finish_kernel(
    tile, storage_ref, tenant_ref, count_ref, inc_down, inc_up, mom_down, mom_up, out_pre, in_pre,
    out_hbm, in_hbm, step_down, step_up, new_down, new_up,
    inc_v, mom_v, step_v, new_v, rows_v, total, row_at, used, tokens, load_sem, store_sem, copy_sem,
):
    slots, seq_count = tenant_ref.shape
    _, owned, rank, width = mom_v.shape
    tiles = width // tile
    s = lax.axis_index("seq")
    tensors = ((inc_down, mom_down, step_down, new_down), (inc_up, mom_up, step_up, new_up))

    def cols(j):
        return pl.ds(j * tile, tile)

    def load(n, j):
        incoming, moment, _, _ = tensors[n]
        return [
            pltpu.make_async_copy(incoming.at[:, :, cols(j)], inc_v.at[n, :, :, cols(j)], load_sem.at[n, j, 0]),
            pltpu.make_async_copy(moment.at[:, :, cols(j)], mom_v.at[n, :, :, cols(j)], load_sem.at[n, j, 1]),
        ]

    def store(n, j):
        _, _, step, new = tensors[n]
        return [
            pltpu.make_async_copy(step_v.at[n, :, :, cols(j)], step.at[:, :, cols(j)], store_sem.at[n, j, 0]),
            pltpu.make_async_copy(new_v.at[n, :, :, cols(j)], new.at[:, :, cols(j)], store_sem.at[n, j, 1]),
        ]

    items = [(n, j) for n in range(2) for j in range(tiles)]
    for n, j in items:
        for cp in load(n, j):
            cp.start()
    takes = [
        pltpu.make_async_copy(in_pre, rows_v.at[0], copy_sem.at[0]),
        pltpu.make_async_copy(out_pre, rows_v.at[1], copy_sem.at[1]),
    ]
    gives = [
        pltpu.make_async_copy(rows_v.at[0], in_hbm, copy_sem.at[2]),
        pltpu.make_async_copy(rows_v.at[1], out_hbm, copy_sem.at[3]),
    ]
    for cp in takes:
        cp.start()

    for k in range(owned):
        tokens[k] = 0

    @pl.loop(0, seq_count)
    def _(i):
        row = jnp.int32(0)
        uses = jnp.int32(0)
        for j in range(slots):
            p = storage_ref[tenant_ref[j, i]]
            here = (p // owned == s).astype(jnp.int32)
            row = row + here * (p % owned)
            uses = uses + here
            tokens[p % owned] = tokens[p % owned] + here * count_ref[j, i]
        row_at[i] = row
        used[i] = uses

    for n, j in items:
        for cp in load(n, j):
            cp.wait()
        total[...] = jnp.zeros_like(total)

        @pl.loop(0, seq_count)
        def _(i):
            @pl.when(used[i] > 0)
            def _():
                k = row_at[i]
                total[k] = total[k] + inc_v[n, i, :, cols(j)].astype(jnp.float32)

        @pl.loop(0, owned)
        def _(k):
            grad = total[k] / jnp.maximum(tokens[k], 1).astype(jnp.float32)
            moment = mom_v[n, k, :, cols(j)]
            combined = beta_first * moment + (1.0 - beta_first) * grad
            spread = jnp.sqrt(jnp.mean(combined * combined, axis=0, keepdims=True) + epsilon)
            step_v[n, k, :, cols(j)] = combined / (jnp.abs(combined) + soft_floor * spread)
            new_v[n, k, :, cols(j)] = beta_second * moment + (1.0 - beta_second) * grad

        for cp in store(n, j):
            cp.start()
        if j == 0:
            takes[n].wait()
            gives[n].start()
    for n, j in items:
        for cp in store(n, j):
            cp.wait()
    for cp in gives:
        cp.wait()


def finish(storage, tenants, counts, inc_down, inc_up, mom_down, mom_up, out_pre, in_pre):
    seq_count, rank, width = inc_down.shape
    owned = mom_down.shape[0]
    tile = min(256, width)
    shape = jax.ShapeDtypeStruct(mom_down.shape, jnp.float32)
    smem = pl.BlockSpec(memory_space=pltpu.SMEM)
    hbm = pl.BlockSpec(memory_space=pl.ANY)
    state = pltpu.VMEM((2, owned, rank, width), jnp.float32)
    return pl.pallas_call(
        functools.partial(finish_kernel, tile),
        out_shape=(
            jax.ShapeDtypeStruct(out_pre.shape, out_pre.dtype), jax.ShapeDtypeStruct(in_pre.shape, in_pre.dtype),
        ) + (shape,) * 4,
        in_specs=[smem] * 3 + [hbm] * 6,
        out_specs=(hbm,) * 6,
        scratch_shapes=[
            pltpu.VMEM((2, seq_count, rank, width), jnp.bfloat16),
            state, state, state,
            pltpu.VMEM((2,) + out_pre.shape, out_pre.dtype),
            pltpu.VMEM((owned, rank, tile), jnp.float32),
            pltpu.SMEM((seq_count,), jnp.int32),
            pltpu.SMEM((seq_count,), jnp.int32),
            pltpu.SMEM((owned,), jnp.int32),
            pltpu.SemaphoreType.DMA((2, width // tile, 2)),
            pltpu.SemaphoreType.DMA((2, width // tile, 2)),
            pltpu.SemaphoreType.DMA((4,)),
        ],
        compiler_params=pltpu.CompilerParams(vmem_limit_bytes=56 * 1024 * 1024),
        name="finish",
    )(storage, tenants, counts, inc_down, inc_up, mom_down, mom_up, out_pre, in_pre)


def local(seq_count, tp_count, x, g, w, down, up, mom_down, mom_up, storage, tenants, counts):
    tenants, counts = tenants.T, counts.T
    out_act, in_grad, inc_down, inc_up = adapter_step(
        storage, tenants, counts, x, g, w, down, up, seq_count, tp_count
    )
    return finish(storage, tenants, counts, inc_down, inc_up, mom_down, mom_up, out_act, in_grad)


def solution(mesh):
    owner = P("seq", None, "tp")
    return jax.shard_map(
        functools.partial(local, mesh.shape["seq"], mesh.shape["tp"]),
        mesh=mesh,
        in_specs=(P("seq", "tp"), P("seq", "tp"), P("tp", None), owner, owner, owner, owner, P(), P(), P()),
        out_specs=(P("seq", "tp"), P("seq", "tp"), owner, owner, owner, owner),
        check_vma=False,
    )
```

```python
import functools

import jax
import jax.numpy as jnp
from jax import lax
from jax.experimental import pallas as pl
from jax.experimental.pallas import tpu as pltpu
from jax.sharding import PartitionSpec as P

adapter_scale = 2.0
beta_first = 0.9
beta_second = 0.99
soft_floor = 0.25
epsilon = 1e-06
contract_last = (((1,), (1,)), ((), ()))
contract_leading = (((0,), (0,)), ((), ()))
MESH = pl.DeviceIdType.MESH
cores = 2


def matmul(a, b, dims=(((1,), (0,)), ((), ()))):
    return lax.dot_general(a, b, dims, preferred_element_type=jnp.float32)


def lion(total, tokens, moment):
    grad = total / jnp.maximum(tokens, 1).astype(jnp.float32)
    combined = beta_first * moment + (1.0 - beta_first) * grad
    spread = jnp.sqrt(jnp.mean(combined * combined, axis=0, keepdims=True) + epsilon)
    step = combined / (jnp.abs(combined) + soft_floor * spread)
    return step, beta_second * moment + (1.0 - beta_second) * grad


def step_kernel(
    seq_count, tp_count, chunks,
    storage_ref, tenant_ref, count_ref, x_hbm, g_hbm, w_hbm, down_hbm, up_hbm, mom_down, mom_up,
    out_v, in_v, inc_up, step_down, new_down, mom_v,
    x_v, w_v, gath, down_v, up_v, send_down, send_up, recv_down, recv_up, slot_down, slot_up,
    part, inc_down, psend_down, psend_up, mine, psib, srecv, acc, mom_down_v, packed, half_recv, half_sum, sum_recv, low_all,
    local_sem, ag_send, ag_recv, a2a_send, a2a_recv, sib_send, sib_recv, sx_send, sx_recv, rank_send, rank_recv, own_sem, row_at, tokens,
):
    s = lax.axis_index("seq")
    t = lax.axis_index("tp")
    chips = tp_count // cores
    chip = t // cores
    core = t % cores
    row_count, width = x_v.shape
    owned, rank, _ = down_v.shape
    slots = slot_down.shape[0] // rank
    sib = {"tp": chip * cores + 1 - core}
    half = row_count // 2
    quarter = half // 2
    step = row_count // chunks
    tile = min(256, width)
    pair = 2 * rank
    part_rows = 64 if step % 64 == 0 else 16

    def tp_of(d, c):
        return lax.rem(chip + d, chips) * cores + c

    def rem_seq(k):
        return lax.rem(s + k, seq_count)

    loads = [
        pltpu.make_async_copy(up_hbm, up_v, local_sem.at[0]),
        pltpu.make_async_copy(down_hbm, down_v, local_sem.at[1]),
        pltpu.make_async_copy(x_hbm, x_v, local_sem.at[2]),
        pltpu.make_async_copy(g_hbm, gath.at[t], local_sem.at[3]),
    ]
    for cp in loads:
        cp.start()
    quarters = []
    for d in list(range(1, chips)) + [0]:
        quarters += [(d, 0), (d, 1)]

    def q_index(d, same):
        return tp_of(d, core if same else 1 - core)

    w_loads = []
    for n, (d, same) in enumerate(quarters):
        q = q_index(d, same)
        cp = pltpu.make_async_copy(
            w_hbm.at[:, pl.ds(pl.multiple_of(q * width, width), width)], w_v.at[q], local_sem.at[4 + n]
        )
        cp.start()
        w_loads.append(cp)

    moments = [
        pltpu.make_async_copy(mom_down, mom_down_v, own_sem.at[2]),
        pltpu.make_async_copy(mom_up, mom_v, own_sem.at[3]),
    ]

    barrier = pltpu.get_barrier_semaphore()
    for k in range(1, seq_count):
        pl.semaphore_signal(barrier, inc=1, device_id={"seq": rem_seq(k)}, device_id_type=MESH)
    for d in range(1, chips):
        pl.semaphore_signal(barrier, inc=1, device_id={"tp": tp_of(d, core)}, device_id_type=MESH)
    pl.semaphore_signal(barrier, inc=1, device_id=sib, device_id_type=MESH)
    pl.semaphore_wait(barrier, seq_count - 1 + chips)

    def rows_of(c):
        return pl.ds(c * step, step)

    def ag(kind, d, c):
        if kind == "sib":
            src, slot, index, to = g_hbm.at[rows_of(c)], t, 0, sib
        elif kind == "chip":
            src, slot, index, to = g_hbm.at[rows_of(c)], t, d, {"tp": tp_of(d, core)}
        else:
            slot = tp_of(chips - d, core)
            src, index, to = gath.at[slot, rows_of(c)], chips - 1 + d, sib
        return pltpu.make_async_remote_copy(
            src_ref=src, dst_ref=gath.at[slot, rows_of(c)], send_sem=ag_send.at[index, c],
            recv_sem=ag_recv.at[index, c], device_id=to, device_id_type=MESH,
        )

    for c in range(chunks):
        for d in range(1, chips):
            ag("chip", d, c).start()
        ag("sib", 0, c).start()

    def forward(c):
        for d in range(1, chips):
            ag("chip", d, c).wait_recv()
            ag("pass", d, c).start()

    def place(i, j):
        return storage_ref[tenant_ref[j, i]]

    def picked(i):
        row = jnp.int32(0)
        for j in range(slots):
            p = place(i, j)
            row = row + jnp.where(p // owned == s, p % owned, 0)
        return row

    def slot_at(owner):
        found = jnp.int32(slots)
        for j in range(slots):
            found = jnp.where(place(s, j) // owned == owner, j, found)
        return found

    def bounds():
        pairs, at = [], jnp.int32(0)
        for j in range(slots):
            pairs.append((at, at + count_ref[j, s]))
            at = at + count_ref[j, s]
        return pairs

    spans = bounds()

    def a2a(n, k, src, dst):
        return pltpu.make_async_remote_copy(
            src_ref=src.at[rem_seq(k)], dst_ref=dst.at[s], send_sem=a2a_send.at[n, k],
            recv_sem=a2a_recv.at[n, k], device_id={"seq": rem_seq(k)}, device_id_type=MESH,
        )

    exchanges = [(send_up, recv_up), (send_down, recv_down), (psend_down, inc_down), (psend_up, inc_up)]

    def pick_send(n, table, send, recv):
        for k in range(1, seq_count):
            j = rem_seq(k)
            send[j] = table[picked(j)]
            a2a(n, k, send, recv).start()
        recv[s] = table[picked(s)]

    loads[0].wait()
    pick_send(0, up_v, send_up, recv_up)
    loads[1].wait()
    pick_send(1, down_v, send_down, recv_down)

    for cp in moments:
        cp.start()

    def sib_copy(d):
        q = q_index(d, 0)
        return pltpu.make_async_remote_copy(
            src_ref=mine.at[q], dst_ref=psib.at[lax.rem(chip + d, chips)], send_sem=sib_send.at[d],
            recv_sem=sib_recv.at[d], device_id=sib, device_id_type=MESH,
        )

    loads[2].wait()
    for n, (d, same) in enumerate(quarters):
        q = q_index(d, same)
        w_loads[n].wait()

        @pl.loop(0, width // tile)
        def _(j):
            cols = pl.ds(pl.multiple_of(j * tile, tile), tile)
            mine[q, :, cols] = matmul(x_v[...], w_v[q, :, cols]).astype(jnp.bfloat16)

        if not same:
            sib_copy(d).start()

    def back_term(slot, first=False):
        @pl.loop(0, width // tile)
        def _(j):
            cols = pl.ds(pl.multiple_of(j * tile, tile), tile)
            term = matmul(gath[slot], w_v[slot, cols, :], contract_last)
            if first:
                acc[:, cols] = term
            else:
                acc[:, cols] = acc[:, cols] + term

    loads[3].wait()
    forward(0)
    back_term(t, True)
    early = max(1, chunks // 2)
    for c in range(1, early - 1):
        forward(c)
    for c in range(chunks):
        ag("sib", 0, c).wait_recv()
    back_term(sib["tp"])
    for c in range(max(1, early - 1), early):
        forward(c)

    def sx(d, c):
        return pltpu.make_async_remote_copy(
            src_ref=mine.at[tp_of(d, core), rows_of(c)], dst_ref=srecv.at[chip, rows_of(c)], send_sem=sx_send.at[d, c],
            recv_sem=sx_recv.at[d, c], device_id={"tp": tp_of(d, core)}, device_id_type=MESH,
        )

    for d in range(1, chips):
        q = tp_of(d, core)
        sib_copy(d).wait_recv()
        for c in range(chunks):
            @pl.loop(0, step // part_rows)
            def _(j):
                rows = pl.ds(pl.multiple_of(c * step + j * part_rows, part_rows), part_rows)
                both = mine[q, rows, :].astype(jnp.float32) + psib[lax.rem(chip + d, chips), rows, :].astype(jnp.float32)
                mine[q, rows, :] = both.astype(jnp.bfloat16)


    def send_sums(begin, end):
        for c in range(begin, end):
            for d in range(1, chips):
                sx(d, c).start()

    block = 64 if half % 64 == 0 else 16
    lane = lax.broadcasted_iota(jnp.int32, (block, pair), 1)
    row_iota = lax.broadcasted_iota(jnp.int32, (block, pair), 0)

    def member(group, first_row):
        lo = jnp.where(lane < rank, spans[2 * group][0], spans[2 * group + 1][0]) - first_row
        hi = jnp.where(lane < rank, spans[2 * group][1], spans[2 * group + 1][1]) - first_row
        return (row_iota >= lo) & (row_iota < hi)

    def gather_slots(recv, slot_v):
        for j in range(slots):
            slot_v[j * rank:(j + 1) * rank] = recv[place(s, j) // owned]

    def project(n, rows_at, slot_v):
        @pl.loop(0, half // block)
        def _(j):
            both = []
            for side in range(2):
                first_row = j * block + side * half
                product = matmul(rows_at(first_row), slot_v[...], contract_last)
                total = jnp.zeros((block, pair), jnp.float32)
                for group in range(slots // 2):
                    total = total + jnp.where(member(group, first_row), product[:, group * pair:(group + 1) * pair], 0.0)
                both.append(total + pltpu.roll(total, rank, 1))
            packed[n, pl.ds(pl.multiple_of(j * block, block), block)] = jnp.where(lane < rank, both[0], both[1]).astype(jnp.bfloat16)

    def rank_copy(n, kind, d=0):
        if kind == "half":
            src, dst, index, to = packed.at[n, pl.ds(pl.multiple_of((1 - core) * quarter, quarter), quarter)], half_recv.at[n], 0, sib
        elif kind == "chip":
            src, dst, index, to = half_sum.at[n], sum_recv.at[n, chip], d, {"tp": tp_of(d, core)}
        else:
            at = pl.ds(pl.multiple_of(core * quarter, quarter), quarter)
            src, dst, index, to = low_all.at[n, at], low_all.at[n, at], chips, sib
        return pltpu.make_async_remote_copy(
            src_ref=src, dst_ref=dst, send_sem=rank_send.at[n, index], recv_sem=rank_recv.at[n, index],
            device_id=to, device_id_type=MESH,
        )

    def reduce_first(n):
        rank_copy(n, "half").start()
        rank_copy(n, "half").wait_recv()
        own = packed[n, pl.ds(pl.multiple_of(core * quarter, quarter), quarter)].astype(jnp.float32)
        half_sum[n] = (own + half_recv[n].astype(jnp.float32)).astype(jnp.bfloat16)
        for d in range(1, chips):
            rank_copy(n, "chip", d).start()

    def reduce_last(n, scale):
        total = half_sum[n].astype(jnp.float32)
        for d in range(1, chips):
            rank_copy(n, "chip", d).wait_recv()
            total = total + sum_recv[n, lax.rem(chip + chips - d, chips)].astype(jnp.float32)
        low_all[n, pl.ds(pl.multiple_of(core * quarter, quarter), quarter)] = (scale * total).astype(jnp.bfloat16)
        rank_copy(n, "whole").start()
        rank_copy(n, "whole").wait_recv()

    def spread(n, j, side):
        values = low_all[n, pl.ds(pl.multiple_of(j * block, block), block)].astype(jnp.float32)
        turned = pltpu.roll(values, rank, 1)
        wide = jnp.where((lane < rank) == (side == 0), values, turned)
        first_row = j * block + side * half
        return jnp.concatenate(
            [jnp.where(member(group, first_row), wide, 0.0).astype(jnp.bfloat16) for group in range(slots // 2)], axis=1
        )

    def spread_into(n, wide_v):
        for side in range(2):
            @pl.loop(0, half // block)
            def _(j):
                wide_v[pl.ds(pl.multiple_of(side * half + j * block, block), block)] = spread(n, j, side)

    part[slots] = jnp.zeros((rank, width), jnp.bfloat16)

    def return_parts(n, wide_v, rows, scale, psend, incoming):
        @pl.loop(0, width // tile)
        def _(j):
            cols = pl.ds(pl.multiple_of(j * tile, tile), tile)
            term = (scale * matmul(wide_v[...], rows[:, cols], contract_leading)).astype(jnp.bfloat16)
            for k in range(slots):
                part[k, :, cols] = term[k * rank:(k + 1) * rank]

        for k in range(1, seq_count):
            j = rem_seq(k)
            psend[j] = part[slot_at(j)]
            a2a(n, k, psend, incoming).start()
        psend[s] = part[slot_at(s)]
        pltpu.make_async_copy(psend.at[s], incoming.at[s], own_sem.at[n - 2]).start()

    def take_parts(n):
        src, dst = exchanges[n]
        pltpu.make_async_copy(src.at[s], dst.at[s], own_sem.at[n - 2]).wait()
        for k in range(1, seq_count):
            a2a(n, k, src, dst).wait_recv()

    def run(wide_grad, wide_low):
        def finish_in():
            @pl.loop(0, width // tile)
            def _(j):
                cols = pl.ds(pl.multiple_of(j * tile, tile), tile)
                in_v[:, cols] = (acc[:, cols] + matmul(wide_grad[...], slot_down[:, cols])).astype(jnp.bfloat16)

        for k in range(1, seq_count):
            a2a(0, k, send_up, recv_up).wait_recv()
        gather_slots(recv_up, slot_up)
        project(0, lambda at: gath[t, pl.ds(pl.multiple_of(at, block), block)], slot_up)
        reduce_first(0)
        send_sums(0, min(2, chunks))
        for c in range(early, chunks):
            forward(c)
        reduce_last(0, adapter_scale)
        spread_into(0, wide_grad)
        return_parts(2, wide_grad, x_v, 1.0, psend_down, inc_down)

        for d in range(1, chips):
            back_term(tp_of(chips - d, core))
        for d in range(1, chips):
            for c in range(chunks):
                ag("pass", d, c).wait_recv()
            back_term(tp_of(chips - d, 1 - core))

        for k in range(1, seq_count):
            a2a(1, k, send_down, recv_down).wait_recv()
        gather_slots(recv_down, slot_down)
        project(1, lambda at: x_v[pl.ds(pl.multiple_of(at, block), block)], slot_down)
        reduce_first(1)
        send_sums(min(2, chunks), chunks)
        finish_in()
        reduce_last(1, 1.0)
        spread_into(1, wide_low)
        return_parts(3, wide_low, gath.at[t], adapter_scale, psend_up, inc_up)

        for cp in moments:
            cp.wait()
        take_parts(2)
        for k in range(owned):
            tokens[k] = 0

        @pl.loop(0, seq_count)
        def _(i):
            row, uses = jnp.int32(0), jnp.int32(0)
            for j in range(slots):
                p = place(i, j)
                here = (p // owned == s).astype(jnp.int32)
                row = row + here * (p % owned)
                uses = uses + here
                for k in range(owned):
                    tokens[k] = tokens[k] + jnp.where(p == s * owned + k, count_ref[j, i], 0)
            row_at[i] = jnp.where(uses > 0, row, -1)

        @pl.loop(0, width // tile)
        def _(j):
            cols = pl.ds(pl.multiple_of(j * tile, tile), tile)
            for k in range(owned):
                def add(i, total):
                    return total + jnp.where(row_at[i] == k, inc_down[i, :, cols].astype(jnp.float32), 0.0)

                total = lax.fori_loop(0, seq_count, add, jnp.zeros((rank, tile), jnp.float32))
                step_down[k, :, cols], new_down[k, :, cols] = lion(total, tokens[k], mom_down_v[k, :, cols])

        sib_copy(0).wait_recv()

        @pl.loop(0, width // tile)
        def _(j):
            cols = pl.ds(pl.multiple_of(j * tile, tile), tile)
            base = mine[t, :, cols].astype(jnp.float32) + psib[chip, :, cols].astype(jnp.float32)
            acc[:, cols] = base + adapter_scale * matmul(wide_low[...], slot_up[:, cols])

        for c in range(chunks):
            for d in range(1, chips):
                sx(d, c).wait_recv()

            @pl.loop(0, step // part_rows)
            def _(j):
                rows = pl.ds(pl.multiple_of(c * step + j * part_rows, part_rows), part_rows)
                total = acc[rows, :]
                for d in range(1, chips):
                    total = total + srecv[lax.rem(chip + chips - d, chips), rows, :].astype(jnp.float32)
                out_v[rows, :] = total.astype(jnp.bfloat16)


    pl.run_scoped(
        run,
        pltpu.VMEM((row_count, slots * rank), jnp.bfloat16),
        pltpu.VMEM((row_count, slots * rank), jnp.bfloat16),
    )

    for c in range(chunks):
        ag("sib", 0, c).wait_send()
        for d in range(1, chips):
            ag("chip", d, c).wait_send()
            ag("pass", d, c).wait_send()
            sx(d, c).wait_send()
    for d in range(chips):
        sib_copy(d).wait_send()
    for n in range(2):
        rank_copy(n, "half").wait_send()
        rank_copy(n, "whole").wait_send()
        for d in range(1, chips):
            rank_copy(n, "chip", d).wait_send()
    for n, (src, dst) in enumerate(exchanges):
        for k in range(1, seq_count):
            a2a(n, k, src, dst).wait_send()
    take_parts(3)


def adapter_step(storage, tenants, counts, x, g, w, down, up, mom_down, mom_up, seq_count, tp_count):
    row_count, width = x.shape
    owned, rank, _ = down.shape
    slots = tenants.shape[0]
    chips = tp_count // cores
    chunks = next(n for n in (6, 3, 2, 1) if row_count % (16 * n) == 0)
    bf16, f32 = jnp.bfloat16, jnp.float32
    dma = pltpu.SemaphoreType.DMA
    smem = pl.BlockSpec(memory_space=pltpu.SMEM)
    hbm = pl.BlockSpec(memory_space=pl.ANY)
    blocks = (seq_count, rank, width)
    vmem = lambda shape, dtype=bf16: pltpu.VMEM(shape, dtype)
    half = row_count // 2
    return pl.pallas_call(
        functools.partial(step_kernel, seq_count, tp_count, chunks),
        out_shape=(
            vmem((row_count, width)),
            vmem((row_count, width)),
            vmem(blocks),
            vmem((owned, rank, width), f32),
            vmem((owned, rank, width), f32),
            vmem((owned, rank, width), f32),
        ),
        in_specs=[smem] * 3 + [hbm] * 7,
        out_specs=(pl.BlockSpec(memory_space=pltpu.VMEM),) * 6,
        scratch_shapes=[
            vmem((row_count, width)),
            vmem((tp_count, width, width)),
            vmem((tp_count, row_count, width)),
            vmem((owned, rank, width)),
            vmem((owned, rank, width)),
            vmem(blocks), vmem(blocks), vmem(blocks), vmem(blocks),
            vmem((slots * rank, width)),
            vmem((slots * rank, width)),
            vmem((slots + 1, rank, width)),
            vmem(blocks), vmem(blocks), vmem(blocks),
            vmem((tp_count, row_count, width)),
            vmem((chips, row_count, width)),
            vmem((chips, row_count, width)),
            vmem((row_count, width), f32),
            vmem((owned, rank, width), f32),
            vmem((2, half, 2 * rank)),
            vmem((2, half // 2, 2 * rank)),
            vmem((2, half // 2, 2 * rank)),
            vmem((2, chips, half // 2, 2 * rank)),
            vmem((2, half, 2 * rank)),
            dma((4 + tp_count,)),
            dma((2 * chips - 1, chunks)), dma((2 * chips - 1, chunks)),
            dma((4, seq_count)), dma((4, seq_count)),
            dma((chips,)), dma((chips,)),
            dma((chips, chunks)), dma((chips, chunks)),
            dma((2, chips + 1)), dma((2, chips + 1)),
            dma((4,)),
            pltpu.SMEM((seq_count,), jnp.int32),
            pltpu.SMEM((owned,), jnp.int32),
        ],
        compiler_params=pltpu.CompilerParams(
            collective_id=0, has_side_effects=True, vmem_limit_bytes=48 * 1024 * 1024
        ),
        name="adapter_step",
    )(storage, tenants, counts, x, g, w, down, up, mom_down, mom_up)


def finish_kernel(
    tile, storage_ref, tenant_ref, count_ref, out_v, in_v, inc_up, step_down_v, new_down_v, mom_v,
    out_hbm, in_hbm, step_down, step_up, new_down, new_up,
    step_v, new_v, total, row_at, used, tokens, store_sem, copy_sem,
):
    slots, seq_count = tenant_ref.shape
    owned, rank, width = mom_v.shape
    tiles = width // tile
    s = lax.axis_index("seq")

    def cols(j):
        return pl.ds(j * tile, tile)

    def store(j):
        return [
            pltpu.make_async_copy(step_v.at[:, :, cols(j)], step_up.at[:, :, cols(j)], store_sem.at[j, 0]),
            pltpu.make_async_copy(new_v.at[:, :, cols(j)], new_up.at[:, :, cols(j)], store_sem.at[j, 1]),
        ]

    copies = [
        pltpu.make_async_copy(src, dst, copy_sem.at[n])
        for n, (src, dst) in enumerate(((out_v, out_hbm), (in_v, in_hbm), (step_down_v, step_down), (new_down_v, new_down)))
    ]
    for cp in copies:
        cp.start()

    for k in range(owned):
        tokens[k] = 0

    @pl.loop(0, seq_count)
    def _(i):
        row = jnp.int32(0)
        uses = jnp.int32(0)
        for j in range(slots):
            p = storage_ref[tenant_ref[j, i]]
            here = (p // owned == s).astype(jnp.int32)
            row = row + here * (p % owned)
            uses = uses + here
            tokens[p % owned] = tokens[p % owned] + here * count_ref[j, i]
        row_at[i] = row
        used[i] = uses

    for j in range(tiles):
        total[...] = jnp.zeros_like(total)

        @pl.loop(0, seq_count)
        def _(i):
            @pl.when(used[i] > 0)
            def _():
                k = row_at[i]
                total[k] = total[k] + inc_up[i, :, cols(j)].astype(jnp.float32)

        @pl.loop(0, owned)
        def _(k):
            step_v[k, :, cols(j)], new_v[k, :, cols(j)] = lion(total[k], tokens[k], mom_v[k, :, cols(j)])

        for cp in store(j):
            cp.start()
    for j in range(tiles):
        for cp in store(j):
            cp.wait()
    for cp in copies:
        cp.wait()


def finish(storage, tenants, counts, out_pre, in_pre, inc_up, step_down, new_down, mom_up):
    seq_count = inc_up.shape[0]
    owned, rank, width = mom_up.shape
    tile = min(256, width)
    shape = jax.ShapeDtypeStruct(mom_up.shape, jnp.float32)
    smem = pl.BlockSpec(memory_space=pltpu.SMEM)
    hbm = pl.BlockSpec(memory_space=pl.ANY)
    state = pltpu.VMEM((owned, rank, width), jnp.float32)
    held = [
        pltpu.with_memory_space_constraint(a, pltpu.VMEM)
        for a in (out_pre, in_pre, inc_up, step_down, new_down, mom_up)
    ]
    return pl.pallas_call(
        functools.partial(finish_kernel, tile),
        out_shape=(
            jax.ShapeDtypeStruct(out_pre.shape, out_pre.dtype), jax.ShapeDtypeStruct(in_pre.shape, in_pre.dtype),
        ) + (shape,) * 4,
        in_specs=[smem] * 3 + [pl.BlockSpec(memory_space=pltpu.VMEM)] * 6,
        out_specs=(hbm,) * 6,
        scratch_shapes=[
            state, state,
            pltpu.VMEM((owned, rank, tile), jnp.float32),
            pltpu.SMEM((seq_count,), jnp.int32),
            pltpu.SMEM((seq_count,), jnp.int32),
            pltpu.SMEM((owned,), jnp.int32),
            pltpu.SemaphoreType.DMA((width // tile, 2)),
            pltpu.SemaphoreType.DMA((4,)),
        ],
        compiler_params=pltpu.CompilerParams(vmem_limit_bytes=48 * 1024 * 1024),
        name="finish",
    )(storage, tenants, counts, *held)


def local(seq_count, tp_count, x, g, w, down, up, mom_down, mom_up, storage, tenants, counts):
    tenants, counts = tenants.T, counts.T
    held = adapter_step(storage, tenants, counts, x, g, w, down, up, mom_down, mom_up, seq_count, tp_count)
    return finish(storage, tenants, counts, *held)


def solution(mesh):
    owner = P("seq", None, "tp")
    return jax.shard_map(
        functools.partial(local, mesh.shape["seq"], mesh.shape["tp"]),
        mesh=mesh,
        in_specs=(P("seq", "tp"), P("seq", "tp"), P("tp", None), owner, owner, owner, owner, P(), P(), P()),
        out_specs=(P("seq", "tp"), P("seq", "tp"), owner, owner, owner, owner),
        check_vma=False,
    )
```

```python
import functools

import jax
import jax.numpy as jnp
from jax import lax
from jax.experimental import pallas as pl
from jax.experimental.pallas import tpu as pltpu
from jax.sharding import PartitionSpec as P

adapter_scale = 2.0
beta_first = 0.9
beta_second = 0.99
soft_floor = 0.25
epsilon = 1e-06
contract_last = (((1,), (1,)), ((), ()))
contract_leading = (((0,), (0,)), ((), ()))
MESH = pl.DeviceIdType.MESH
cores = 2
wide_of = 2


def matmul(a, b, dims=(((1,), (0,)), ((), ()))):
    return lax.dot_general(a, b, dims, preferred_element_type=jnp.float32)


def lion(total, tokens, moment):
    grad = total / jnp.maximum(tokens, 1).astype(jnp.float32)
    combined = beta_first * moment + (1.0 - beta_first) * grad
    spread = jnp.sqrt(jnp.mean(combined * combined, axis=0, keepdims=True) + epsilon)
    step = combined / (jnp.abs(combined) + soft_floor * spread)
    return step, beta_second * moment + (1.0 - beta_second) * grad


def step_kernel(
    relayed, seq_count, tp_count, chunks,
    storage_ref, tenant_ref, count_ref, x_hbm, g_hbm, w_hbm, down_hbm, up_hbm, mom_down, mom_up,
    out_v, in_v, inc_up, step_down, new_down, mom_v,
    x_v, w_v, gath, down_v, up_v, send_down, send_up, recv_down, recv_up, slot_down, slot_up,
    part, inc_down, psend_down, psend_up, mine, psib, srecv, acc, mom_down_v, packed, half_recv, half_sum, sum_recv, low_all,
    local_sem, ag_send, ag_recv, a2a_send, a2a_recv, sib_send, sib_recv, sx_send, sx_recv, rank_send, rank_recv, own_sem, row_at, tokens, *relay_refs,
):
    s = lax.axis_index("seq")
    t = lax.axis_index("tp")
    chips = tp_count // cores
    chip = t // cores
    core = t % cores
    row_count, width = x_v.shape
    owned, rank, _ = down_v.shape
    slots = slot_down.shape[0] // rank
    sib = {"tp": chip * cores + 1 - core}
    half = row_count // 2
    quarter = half // 2
    step = row_count // chunks
    tile = min(256, width)
    pair = 2 * rank
    part_rows = 64 if step % 64 == 0 else 16

    def tp_of(d, c):
        return lax.rem(chip + d, chips) * cores + c

    def peer(k):
        if seq_count & (seq_count - 1):
            return lax.rem(s + k, seq_count)
        at = s
        for bit in range(seq_count.bit_length() - 1):
            if k >> bit & 1:
                at = at + (1 << bit) * (1 - 2 * (s // (1 << bit) % 2))
        return at

    loads = [
        pltpu.make_async_copy(up_hbm, up_v, local_sem.at[0]),
        pltpu.make_async_copy(down_hbm, down_v, local_sem.at[1]),
        pltpu.make_async_copy(x_hbm, x_v, local_sem.at[2]),
        pltpu.make_async_copy(g_hbm, gath.at[t], local_sem.at[3]),
    ]
    for cp in loads:
        cp.start()
    quarters = []
    for d in list(range(1, chips)) + [0]:
        quarters += [(d, 0), (d, 1)]

    def q_index(d, same):
        return tp_of(d, core if same else 1 - core)

    w_loads = []
    for n, (d, same) in enumerate(quarters):
        q = q_index(d, same)
        cp = pltpu.make_async_copy(
            w_hbm.at[:, pl.ds(pl.multiple_of(q * width, width), width)], w_v.at[q], local_sem.at[4 + n]
        )
        cp.start()
        w_loads.append(cp)

    moments = [
        pltpu.make_async_copy(mom_down, mom_down_v, own_sem.at[2]),
        pltpu.make_async_copy(mom_up, mom_v, own_sem.at[3]),
    ]

    barrier = pltpu.get_barrier_semaphore()
    for k in range(1, seq_count):
        pl.semaphore_signal(barrier, inc=1, device_id={"seq": peer(k)}, device_id_type=MESH)
    for d in range(1, chips):
        pl.semaphore_signal(barrier, inc=1, device_id={"tp": tp_of(d, core)}, device_id_type=MESH)
    pl.semaphore_signal(barrier, inc=1, device_id=sib, device_id_type=MESH)
    pl.semaphore_wait(barrier, seq_count - 1 + chips)

    def rows_of(c):
        return pl.ds(c * step, step)

    def ag(kind, d, c):
        if kind == "sib":
            src, slot, index, to = g_hbm.at[rows_of(c)], t, 0, sib
        elif kind == "chip":
            src, slot, index, to = g_hbm.at[rows_of(c)], t, d, {"tp": tp_of(d, core)}
        else:
            slot = tp_of(chips - d, core)
            src, index, to = gath.at[slot, rows_of(c)], chips - 1 + d, sib
        return pltpu.make_async_remote_copy(
            src_ref=src, dst_ref=gath.at[slot, rows_of(c)], send_sem=ag_send.at[index, c],
            recv_sem=ag_recv.at[index, c], device_id=to, device_id_type=MESH,
        )

    for c in range(chunks):
        for d in range(1, chips):
            ag("chip", d, c).start()
        ag("sib", 0, c).start()

    def forward(c):
        for d in range(1, chips):
            ag("chip", d, c).wait_recv()
            ag("pass", d, c).start()

    def place(i, j):
        return storage_ref[tenant_ref[j, i]]

    def picked(i):
        row = jnp.int32(0)
        for j in range(slots):
            p = place(i, j)
            row = row + jnp.where(p // owned == s, p % owned, 0)
        return row

    def slot_at(owner):
        found = jnp.int32(slots)
        for j in range(slots):
            found = jnp.where(place(s, j) // owned == owner, j, found)
        return found

    def bounds():
        pairs, at = [], jnp.int32(0)
        for j in range(slots):
            pairs.append((at, at + count_ref[j, s]))
            at = at + count_ref[j, s]
        return pairs

    spans = bounds()

    def a2a(n, k, src, dst):
        return pltpu.make_async_remote_copy(
            src_ref=src.at[peer(k)], dst_ref=dst.at[s], send_sem=a2a_send.at[n, k],
            recv_sem=a2a_recv.at[n, k], device_id={"seq": peer(k)}, device_id_type=MESH,
        )

    exchanges = [(send_up, recv_up), (send_down, recv_down), (psend_down, inc_down), (psend_up, inc_up)]

    def pick_send(n, table, send, recv):
        for k in range(1, seq_count):
            j = peer(k)
            send[j] = table[picked(j)]
            a2a(n, k, send, recv).start()
        recv[s] = table[picked(s)]

    side_count = seq_count // 2
    side = s // side_count
    mirror = seq_count - wide_of
    near = range(1, side_count)
    far = range(side_count, seq_count)

    def owner_of(i, j):
        return place(i, j) // owned

    def needs(i, owner):
        hit = jnp.int32(0)
        for j in range(slots):
            hit = hit + (owner_of(i, j) == owner).astype(jnp.int32)
        return hit

    def any_gap(flags, upto):
        full = jnp.int32(0)
        for flag in flags[:upto]:
            full = full + flag
        return (full < upto).astype(jnp.int32)

    def packed_at(flags, c):
        before = jnp.int32(0)
        for n, flag in enumerate(flags):
            before = before + jnp.where(n < c, flag, 0)
        return jnp.clip(c - (before < c).astype(jnp.int32), 0, slots - 2)

    if relayed:
        via, cand, mid_send, parts_send, parts_held, owner_send, cand_send, cand_recv, mid_sem, mid_recv, parts_sem, parts_recv, owner_sem = relay_refs

        def mirrored(k):
            return peer(k ^ mirror)

        def to_relay(k):
            return pltpu.make_async_remote_copy(
                src_ref=via.at[k], dst_ref=cand.at[s % side_count], send_sem=cand_send.at[k], recv_sem=cand_recv.at[k],
                device_id={"seq": peer(k)}, device_id_type=MESH,
            )

        def across(j):
            return pltpu.make_async_remote_copy(
                src_ref=mid_send.at[j], dst_ref=recv_down.at[seq_count + j], send_sem=mid_sem.at[j],
                recv_sem=mid_recv.at[j], device_id={"seq": peer(mirror)}, device_id_type=MESH,
            )

        def relay_maps():
            for k in near:
                to_relay(k).wait_recv()
            flags = [needs(peer(mirror), side * side_count + c) for c in range(side_count)]
            for j in range(slots - 1):
                mid_send[j] = cand[j + any_gap(flags, j + 1)]
                across(j).start()

        def parts_copy(j):
            return pltpu.make_async_remote_copy(
                src_ref=parts_send.at[j], dst_ref=parts_held.at[j], send_sem=parts_sem.at[j],
                recv_sem=parts_recv.at[j], device_id={"seq": peer(mirror)}, device_id_type=MESH,
            )

        def owner_copy(k):
            return pltpu.make_async_remote_copy(
                src_ref=owner_send.at[k], dst_ref=inc_down.at[peer(mirror)], send_sem=owner_sem.at[k],
                recv_sem=a2a_recv.at[2, k ^ mirror], device_id={"seq": peer(k)}, device_id_type=MESH,
            )

        def relay_parts():
            for j in range(slots - 1):
                parts_copy(j).wait_recv()
            source = peer(mirror)
            flags = [(owner_of(source, j) // side_count == side).astype(jnp.int32) for j in range(slots)]

            def term(o):
                slot = jnp.int32(0)
                for j in range(slots):
                    slot = slot + jnp.where(owner_of(source, j) == o, j, 0)
                return parts_held[packed_at(flags, slot)]

            for k in near:
                owner_send[k] = term(peer(k))
                owner_copy(k).start()
            inc_down[source] = term(s)

    if relayed:
        loads[1].wait()
        for k in near:
            via[k] = down_v[picked(mirrored(k))]
            to_relay(k).start()
        cand[s % side_count] = down_v[picked(peer(mirror))]

        loads[0].wait()
        pick_send(0, up_v, send_up, recv_up)
        for k in near:
            send_down[peer(k)] = down_v[picked(peer(k))]
            a2a(1, k, send_down, recv_down).start()
        recv_down[s] = down_v[picked(s)]
    else:
        loads[0].wait()
        pick_send(0, up_v, send_up, recv_up)
        loads[1].wait()
        pick_send(1, down_v, send_down, recv_down)

    for cp in moments:
        cp.start()

    def sib_copy(d):
        q = q_index(d, 0)
        return pltpu.make_async_remote_copy(
            src_ref=mine.at[q], dst_ref=psib.at[lax.rem(chip + d, chips)], send_sem=sib_send.at[d],
            recv_sem=sib_recv.at[d], device_id=sib, device_id_type=MESH,
        )

    loads[2].wait()
    for n, (d, same) in enumerate(quarters):
        q = q_index(d, same)
        w_loads[n].wait()

        @pl.loop(0, width // tile)
        def _(j):
            cols = pl.ds(pl.multiple_of(j * tile, tile), tile)
            mine[q, :, cols] = matmul(x_v[...], w_v[q, :, cols]).astype(jnp.bfloat16)

        if not same:
            sib_copy(d).start()

    def back_term(slot, first=False):
        @pl.loop(0, width // tile)
        def _(j):
            cols = pl.ds(pl.multiple_of(j * tile, tile), tile)
            term = matmul(gath[slot], w_v[slot, cols, :], contract_last)
            if first:
                acc[:, cols] = term
            else:
                acc[:, cols] = acc[:, cols] + term

    loads[3].wait()
    forward(0)
    back_term(t, True)
    early = max(1, chunks // 2)
    for c in range(1, early - 1):
        forward(c)
    for c in range(chunks):
        ag("sib", 0, c).wait_recv()
    if relayed:
        relay_maps()
    back_term(sib["tp"])
    for c in range(max(1, early - 1), early):
        forward(c)

    def sx(d, c):
        return pltpu.make_async_remote_copy(
            src_ref=mine.at[tp_of(d, core), rows_of(c)], dst_ref=srecv.at[chip, rows_of(c)], send_sem=sx_send.at[d, c],
            recv_sem=sx_recv.at[d, c], device_id={"tp": tp_of(d, core)}, device_id_type=MESH,
        )

    for d in range(1, chips):
        q = tp_of(d, core)
        sib_copy(d).wait_recv()
        for c in range(chunks):
            @pl.loop(0, step // part_rows)
            def _(j):
                rows = pl.ds(pl.multiple_of(c * step + j * part_rows, part_rows), part_rows)
                both = mine[q, rows, :].astype(jnp.float32) + psib[lax.rem(chip + d, chips), rows, :].astype(jnp.float32)
                mine[q, rows, :] = both.astype(jnp.bfloat16)


    def send_sums(begin, end):
        for c in range(begin, end):
            for d in range(1, chips):
                sx(d, c).start()

    block = next(n for n in (192, 128, 64, 16) if half % n == 0)
    lane = lax.broadcasted_iota(jnp.int32, (block, pair), 1)
    row_iota = lax.broadcasted_iota(jnp.int32, (block, pair), 0)

    def member(group, first_row):
        lo = jnp.where(lane < rank, spans[2 * group][0], spans[2 * group + 1][0]) - first_row
        hi = jnp.where(lane < rank, spans[2 * group][1], spans[2 * group + 1][1]) - first_row
        return (row_iota >= lo) & (row_iota < hi)

    def gather_slots(recv, slot_v, apart=False):
        for j in range(slots):
            at = owner_of(s, j)
            if apart:
                flags = [needs(s, (1 - side) * side_count + c) for c in range(side_count)]
                at = jnp.where(at // side_count == side, at, seq_count + packed_at(flags, at % side_count))
            slot_v[j * rank:(j + 1) * rank] = recv[at]

    def project(n, rows_at, slot_v):
        @pl.loop(0, half // block)
        def _(j):
            both = []
            for side in range(2):
                first_row = j * block + side * half
                product = matmul(rows_at(first_row), slot_v[...], contract_last)
                total = jnp.zeros((block, pair), jnp.float32)
                for group in range(slots // 2):
                    total = total + jnp.where(member(group, first_row), product[:, group * pair:(group + 1) * pair], 0.0)
                both.append(total + pltpu.roll(total, rank, 1))
            packed[n, pl.ds(pl.multiple_of(j * block, block), block)] = jnp.where(lane < rank, both[0], both[1]).astype(jnp.bfloat16)

    def rank_copy(n, kind, d=0):
        if kind == "half":
            src, dst, index, to = packed.at[n, pl.ds(pl.multiple_of((1 - core) * quarter, quarter), quarter)], half_recv.at[n], 0, sib
        elif kind == "chip":
            src, dst, index, to = half_sum.at[n], sum_recv.at[n, chip], d, {"tp": tp_of(d, core)}
        else:
            at = pl.ds(pl.multiple_of(core * quarter, quarter), quarter)
            src, dst, index, to = low_all.at[n, at], low_all.at[n, at], chips, sib
        return pltpu.make_async_remote_copy(
            src_ref=src, dst_ref=dst, send_sem=rank_send.at[n, index], recv_sem=rank_recv.at[n, index],
            device_id=to, device_id_type=MESH,
        )

    def reduce_first(n):
        rank_copy(n, "half").start()
        rank_copy(n, "half").wait_recv()
        own = packed[n, pl.ds(pl.multiple_of(core * quarter, quarter), quarter)].astype(jnp.float32)
        half_sum[n] = (own + half_recv[n].astype(jnp.float32)).astype(jnp.bfloat16)
        for d in range(1, chips):
            rank_copy(n, "chip", d).start()

    def reduce_last(n, scale):
        total = half_sum[n].astype(jnp.float32)
        for d in range(1, chips):
            rank_copy(n, "chip", d).wait_recv()
            total = total + sum_recv[n, lax.rem(chip + chips - d, chips)].astype(jnp.float32)
        low_all[n, pl.ds(pl.multiple_of(core * quarter, quarter), quarter)] = (scale * total).astype(jnp.bfloat16)
        rank_copy(n, "whole").start()
        rank_copy(n, "whole").wait_recv()

    def spread(n, j, side):
        values = low_all[n, pl.ds(pl.multiple_of(j * block, block), block)].astype(jnp.float32)
        turned = pltpu.roll(values, rank, 1)
        wide = jnp.where((lane < rank) == (side == 0), values, turned)
        first_row = j * block + side * half
        return jnp.concatenate(
            [jnp.where(member(group, first_row), wide, 0.0).astype(jnp.bfloat16) for group in range(slots // 2)], axis=1
        )

    def spread_into(n, wide_v):
        for side in range(2):
            @pl.loop(0, half // block)
            def _(j):
                wide_v[pl.ds(pl.multiple_of(side * half + j * block, block), block)] = spread(n, j, side)

    part[slots] = jnp.zeros((rank, width), jnp.bfloat16)

    def return_parts(n, wide_v, rows, scale, psend, incoming):
        @pl.loop(0, width // tile)
        def _(j):
            cols = pl.ds(pl.multiple_of(j * tile, tile), tile)
            term = (scale * matmul(wide_v[...], rows[:, cols], contract_leading)).astype(jnp.bfloat16)
            for k in range(slots):
                part[k, :, cols] = term[k * rank:(k + 1) * rank]

        if relayed and n == 2:
            flags = [(owner_of(s, j) // side_count != side).astype(jnp.int32) for j in range(slots)]
            for j in range(slots - 1):
                parts_send[j] = part[j + any_gap(flags, j + 1)]
                parts_copy(j).start()
        for k in near if relayed and n == 2 else range(1, seq_count):
            j = peer(k)
            psend[j] = part[slot_at(j)]
            a2a(n, k, psend, incoming).start()
        psend[s] = part[slot_at(s)]
        pltpu.make_async_copy(psend.at[s], incoming.at[s], own_sem.at[n - 2]).start()

    def take_parts(n):
        src, dst = exchanges[n]
        pltpu.make_async_copy(src.at[s], dst.at[s], own_sem.at[n - 2]).wait()
        for k in range(1, seq_count):
            if not (relayed and n == 2 and k == mirror):
                a2a(n, k, src, dst).wait_recv()

    def run(wide_grad, wide_low):
        def finish_in():
            @pl.loop(0, width // tile)
            def _(j):
                cols = pl.ds(pl.multiple_of(j * tile, tile), tile)
                in_v[:, cols] = (acc[:, cols] + matmul(wide_grad[...], slot_down[:, cols])).astype(jnp.bfloat16)

        for k in range(1, seq_count):
            a2a(0, k, send_up, recv_up).wait_recv()
        gather_slots(recv_up, slot_up)
        project(0, lambda at: gath[t, pl.ds(pl.multiple_of(at, block), block)], slot_up)
        reduce_first(0)
        send_sums(0, min(2, chunks))
        for c in range(early, chunks):
            forward(c)
        reduce_last(0, adapter_scale)
        spread_into(0, wide_grad)
        return_parts(2, wide_grad, x_v, 1.0, psend_down, inc_down)

        for d in range(1, chips):
            back_term(tp_of(chips - d, core))
        for d in range(1, chips):
            for c in range(chunks):
                ag("pass", d, c).wait_recv()
            back_term(tp_of(chips - d, 1 - core))

        for k in near if relayed else range(1, seq_count):
            a2a(1, k, send_down, recv_down).wait_recv()
        if relayed:
            for j in range(slots - 1):
                across(j).wait_recv()
        gather_slots(recv_down, slot_down, relayed)
        project(1, lambda at: x_v[pl.ds(pl.multiple_of(at, block), block)], slot_down)
        reduce_first(1)
        send_sums(min(2, chunks), chunks)
        finish_in()
        reduce_last(1, 1.0)
        spread_into(1, wide_low)
        if relayed:
            relay_parts()
        return_parts(3, wide_low, gath.at[t], adapter_scale, psend_up, inc_up)

        sib_copy(0).wait_recv()

        @pl.loop(0, width // tile)
        def _(j):
            cols = pl.ds(pl.multiple_of(j * tile, tile), tile)
            base = mine[t, :, cols].astype(jnp.float32) + psib[chip, :, cols].astype(jnp.float32)
            acc[:, cols] = base + adapter_scale * matmul(wide_low[...], slot_up[:, cols])

        for c in range(chunks):
            for d in range(1, chips):
                sx(d, c).wait_recv()

            @pl.loop(0, step // part_rows)
            def _(j):
                rows = pl.ds(pl.multiple_of(c * step + j * part_rows, part_rows), part_rows)
                total = acc[rows, :]
                for d in range(1, chips):
                    total = total + srecv[lax.rem(chip + chips - d, chips), rows, :].astype(jnp.float32)
                out_v[rows, :] = total.astype(jnp.bfloat16)

        for cp in moments:
            cp.wait()
        take_parts(2)
        for k in range(owned):
            tokens[k] = 0

        @pl.loop(0, seq_count)
        def _(i):
            row, uses = jnp.int32(0), jnp.int32(0)
            for j in range(slots):
                p = place(i, j)
                here = (p // owned == s).astype(jnp.int32)
                row = row + here * (p % owned)
                uses = uses + here
                for k in range(owned):
                    tokens[k] = tokens[k] + jnp.where(p == s * owned + k, count_ref[j, i], 0)
            row_at[i] = jnp.where(uses > 0, row, -1)

        @pl.loop(0, width // tile)
        def _(j):
            cols = pl.ds(pl.multiple_of(j * tile, tile), tile)
            for k in range(owned):
                def add(i, total):
                    return total + jnp.where(row_at[i] == k, inc_down[i, :, cols].astype(jnp.float32), 0.0)

                total = lax.fori_loop(0, seq_count, add, jnp.zeros((rank, tile), jnp.float32))
                step_down[k, :, cols], new_down[k, :, cols] = lion(total, tokens[k], mom_down_v[k, :, cols])

    pl.run_scoped(
        run,
        pltpu.VMEM((row_count, slots * rank), jnp.bfloat16),
        pltpu.VMEM((row_count, slots * rank), jnp.bfloat16),
    )

    for c in range(chunks):
        ag("sib", 0, c).wait_send()
        for d in range(1, chips):
            ag("chip", d, c).wait_send()
            ag("pass", d, c).wait_send()
            sx(d, c).wait_send()
    for d in range(chips):
        sib_copy(d).wait_send()
    for n in range(2):
        rank_copy(n, "half").wait_send()
        rank_copy(n, "whole").wait_send()
        for d in range(1, chips):
            rank_copy(n, "chip", d).wait_send()
    for n, (src, dst) in enumerate(exchanges):
        for k in range(1, seq_count):
            if not (relayed and n in (1, 2) and k in far):
                a2a(n, k, src, dst).wait_send()
    if relayed:
        for j in range(slots - 1):
            parts_copy(j).wait_send()
            across(j).wait_send()
        for k in near:
            to_relay(k).wait_send()
            owner_copy(k).wait_send()
    take_parts(3)


def adapter_step(storage, tenants, counts, x, g, w, down, up, mom_down, mom_up, seq_count, tp_count, relayed):
    row_count, width = x.shape
    owned, rank, _ = down.shape
    slots = tenants.shape[0]
    chips = tp_count // cores
    chunks = next(n for n in (6, 3, 2, 1) if row_count % (16 * n) == 0)
    bf16, f32 = jnp.bfloat16, jnp.float32
    dma = pltpu.SemaphoreType.DMA
    smem = pl.BlockSpec(memory_space=pltpu.SMEM)
    hbm = pl.BlockSpec(memory_space=pl.ANY)
    blocks = (seq_count, rank, width)
    vmem = lambda shape, dtype=bf16: pltpu.VMEM(shape, dtype)
    half = row_count // 2
    few = slots - 1
    sides = (seq_count // 2, rank, width)
    relay_scratch = [
        vmem(sides), vmem(sides), vmem((few, rank, width)), vmem((few, rank, width)), vmem((few, rank, width)), vmem(sides),
        dma((seq_count // 2,)), dma((seq_count // 2,)), dma((few,)), dma((few,)), dma((few,)), dma((few,)), dma((seq_count // 2,)),
    ]
    return pl.pallas_call(
        functools.partial(step_kernel, relayed, seq_count, tp_count, chunks),
        out_shape=(
            vmem((row_count, width)),
            vmem((row_count, width)),
            vmem(blocks),
            vmem((owned, rank, width), f32),
            vmem((owned, rank, width), f32),
            vmem((owned, rank, width), f32),
        ),
        in_specs=[smem] * 3 + [hbm] * 7,
        out_specs=(pl.BlockSpec(memory_space=pltpu.VMEM),) * 6,
        scratch_shapes=[
            vmem((row_count, width)),
            vmem((tp_count, width, width)),
            vmem((tp_count, row_count, width)),
            vmem((owned, rank, width)),
            vmem((owned, rank, width)),
            vmem(blocks), vmem(blocks), vmem((seq_count + slots - 1, rank, width)), vmem(blocks),
            vmem((slots * rank, width)),
            vmem((slots * rank, width)),
            vmem((slots + 1, rank, width)),
            vmem(blocks), vmem(blocks), vmem(blocks),
            vmem((tp_count, row_count, width)),
            vmem((chips, row_count, width)),
            vmem((chips, row_count, width)),
            vmem((row_count, width), f32),
            vmem((owned, rank, width), f32),
            vmem((2, half, 2 * rank)),
            vmem((2, half // 2, 2 * rank)),
            vmem((2, half // 2, 2 * rank)),
            vmem((2, chips, half // 2, 2 * rank)),
            vmem((2, half, 2 * rank)),
            dma((4 + tp_count,)),
            dma((2 * chips - 1, chunks)), dma((2 * chips - 1, chunks)),
            dma((4, seq_count)), dma((4, seq_count)),
            dma((chips,)), dma((chips,)),
            dma((chips, chunks)), dma((chips, chunks)),
            dma((2, chips + 1)), dma((2, chips + 1)),
            dma((4,)),
            pltpu.SMEM((seq_count,), jnp.int32),
            pltpu.SMEM((owned,), jnp.int32),
        ] + (relay_scratch if relayed else []),
        compiler_params=pltpu.CompilerParams(
            collective_id=1 if relayed else 0, has_side_effects=True, vmem_limit_bytes=52 * 1024 * 1024
        ),
        name="adapter_step_packed" if relayed else "adapter_step",
    )(storage, tenants, counts, x, g, w, down, up, mom_down, mom_up)


def most_kernel(side_rows, storage_ref, tenant_ref, out_ref):
    slots, seq_count = tenant_ref.shape
    most = jnp.int32(0)
    for i in range(seq_count):
        across = jnp.int32(0)
        for j in range(slots):
            high = storage_ref[tenant_ref[j, i]] >= side_rows
            across = across + (high != (i >= seq_count // 2)).astype(jnp.int32)
        most = jnp.maximum(most, across)
    out_ref[0] = most


def most_across(storage, tenants, owned):
    smem = pl.BlockSpec(memory_space=pltpu.SMEM)
    return pl.pallas_call(
        functools.partial(most_kernel, owned * (tenants.shape[1] // 2)),
        out_shape=jax.ShapeDtypeStruct((1,), jnp.int32),
        in_specs=[smem, smem],
        out_specs=smem,
        name="most_across",
    )(storage, tenants)


def finish_kernel(
    tile, storage_ref, tenant_ref, count_ref, out_v, in_v, inc_up, step_down_v, new_down_v, mom_v,
    out_hbm, in_hbm, step_down, step_up, new_down, new_up,
    step_v, new_v, total, row_at, used, tokens, store_sem, copy_sem,
):
    slots, seq_count = tenant_ref.shape
    owned, rank, width = mom_v.shape
    tiles = width // tile
    s = lax.axis_index("seq")

    def cols(j):
        return pl.ds(j * tile, tile)

    def store(j):
        return [
            pltpu.make_async_copy(step_v.at[:, :, cols(j)], step_up.at[:, :, cols(j)], store_sem.at[j, 0]),
            pltpu.make_async_copy(new_v.at[:, :, cols(j)], new_up.at[:, :, cols(j)], store_sem.at[j, 1]),
        ]

    copies = [
        pltpu.make_async_copy(src, dst, copy_sem.at[n])
        for n, (src, dst) in enumerate(((out_v, out_hbm), (in_v, in_hbm), (step_down_v, step_down), (new_down_v, new_down)))
    ]
    for cp in copies:
        cp.start()

    for k in range(owned):
        tokens[k] = 0

    @pl.loop(0, seq_count)
    def _(i):
        row = jnp.int32(0)
        uses = jnp.int32(0)
        for j in range(slots):
            p = storage_ref[tenant_ref[j, i]]
            here = (p // owned == s).astype(jnp.int32)
            row = row + here * (p % owned)
            uses = uses + here
            tokens[p % owned] = tokens[p % owned] + here * count_ref[j, i]
        row_at[i] = row
        used[i] = uses

    for j in range(tiles):
        total[...] = jnp.zeros_like(total)

        @pl.loop(0, seq_count)
        def _(i):
            @pl.when(used[i] > 0)
            def _():
                k = row_at[i]
                total[k] = total[k] + inc_up[i, :, cols(j)].astype(jnp.float32)

        @pl.loop(0, owned)
        def _(k):
            step_v[k, :, cols(j)], new_v[k, :, cols(j)] = lion(total[k], tokens[k], mom_v[k, :, cols(j)])

        for cp in store(j):
            cp.start()
    for j in range(tiles):
        for cp in store(j):
            cp.wait()
    for cp in copies:
        cp.wait()


def finish(storage, tenants, counts, out_pre, in_pre, inc_up, step_down, new_down, mom_up):
    seq_count = inc_up.shape[0]
    owned, rank, width = mom_up.shape
    tile = min(256, width)
    shape = jax.ShapeDtypeStruct(mom_up.shape, jnp.float32)
    smem = pl.BlockSpec(memory_space=pltpu.SMEM)
    hbm = pl.BlockSpec(memory_space=pl.ANY)
    state = pltpu.VMEM((owned, rank, width), jnp.float32)
    held = [
        pltpu.with_memory_space_constraint(a, pltpu.VMEM)
        for a in (out_pre, in_pre, inc_up, step_down, new_down, mom_up)
    ]
    return pl.pallas_call(
        functools.partial(finish_kernel, tile),
        out_shape=(
            jax.ShapeDtypeStruct(out_pre.shape, out_pre.dtype), jax.ShapeDtypeStruct(in_pre.shape, in_pre.dtype),
        ) + (shape,) * 4,
        in_specs=[smem] * 3 + [pl.BlockSpec(memory_space=pltpu.VMEM)] * 6,
        out_specs=(hbm,) * 6,
        scratch_shapes=[
            state, state,
            pltpu.VMEM((owned, rank, tile), jnp.float32),
            pltpu.SMEM((seq_count,), jnp.int32),
            pltpu.SMEM((seq_count,), jnp.int32),
            pltpu.SMEM((owned,), jnp.int32),
            pltpu.SemaphoreType.DMA((width // tile, 2)),
            pltpu.SemaphoreType.DMA((4,)),
        ],
        compiler_params=pltpu.CompilerParams(vmem_limit_bytes=48 * 1024 * 1024),
        name="finish",
    )(storage, tenants, counts, *held)


def local(seq_count, tp_count, x, g, w, down, up, mom_down, mom_up, storage, tenants, counts):
    tenants, counts = tenants.T, counts.T

    def steps(relayed, *operands):
        held = adapter_step(*operands, seq_count, tp_count, relayed)
        return finish(*operands[:3], *held)

    operands = (storage, tenants, counts, x, g, w, down, up, mom_down, mom_up)
    slots, owned = tenants.shape[0], down.shape[0]
    if seq_count != 8 or slots != seq_count // 2:
        return steps(False, *operands)
    return lax.cond(
        most_across(storage, tenants, owned)[0] < slots, functools.partial(steps, True), functools.partial(steps, False), *operands
    )


def solution(mesh):
    owner = P("seq", None, "tp")
    return jax.shard_map(
        functools.partial(local, mesh.shape["seq"], mesh.shape["tp"]),
        mesh=mesh,
        in_specs=(P("seq", "tp"), P("seq", "tp"), P("tp", None), owner, owner, owner, owner, P(), P(), P()),
        out_specs=(P("seq", "tp"), P("seq", "tp"), owner, owner, owner, owner),
        check_vma=False,
    )
```

```python
import functools

import jax
import jax.numpy as jnp
from jax import lax
from jax.experimental import pallas as pl
from jax.experimental.pallas import tpu as pltpu
from jax.sharding import PartitionSpec as P

adapter_scale = 2.0
beta_first = 0.9
beta_second = 0.99
soft_floor = 0.25
epsilon = 1e-06
contract_last = (((1,), (1,)), ((), ()))
contract_leading = (((0,), (0,)), ((), ()))
MESH = pl.DeviceIdType.MESH
cores = 2
wide_of = 2


def matmul(a, b, dims=(((1,), (0,)), ((), ()))):
    return lax.dot_general(a, b, dims, preferred_element_type=jnp.float32)


def lion(total, tokens, moment):
    grad = total / jnp.maximum(tokens, 1).astype(jnp.float32)
    combined = beta_first * moment + (1.0 - beta_first) * grad
    spread = jnp.sqrt(jnp.mean(combined * combined, axis=0, keepdims=True) + epsilon)
    step = combined / (jnp.abs(combined) + soft_floor * spread)
    return step, beta_second * moment + (1.0 - beta_second) * grad


def step_kernel(
    relayed, seq_count, tp_count, chunks,
    storage_ref, tenant_ref, count_ref, x_hbm, g_hbm, w_hbm, down_hbm, up_hbm, mom_down, mom_up,
    out_v, in_v, inc_up, step_down, new_down, mom_v,
    x_v, w_v, gath, down_v, up_v, send_down, send_up, recv_down, recv_up, slot_down, slot_up,
    part, inc_down, psend_down, psend_up, mine, psib, srecv, acc, mom_down_v, packed, half_recv, half_sum, sum_recv, low_all,
    local_sem, ag_send, ag_recv, a2a_send, a2a_recv, sib_send, sib_recv, sx_send, sx_recv, rank_send, rank_recv, own_sem, row_at, tokens, *relay_refs,
):
    s = lax.axis_index("seq")
    t = lax.axis_index("tp")
    chips = tp_count // cores
    chip = t // cores
    core = t % cores
    row_count, width = x_v.shape
    owned, rank, _ = down_v.shape
    slots = slot_down.shape[0] // rank
    sib = {"tp": chip * cores + 1 - core}
    half = row_count // 2
    quarter = half // 2
    step = row_count // chunks
    tile = min(256, width)
    pair = 2 * rank
    part_rows = 64 if step % 64 == 0 else 16

    def tp_of(d, c):
        return lax.rem(chip + d, chips) * cores + c

    def peer(k):
        if seq_count & (seq_count - 1):
            return lax.rem(s + k, seq_count)
        at = s
        for bit in range(seq_count.bit_length() - 1):
            if k >> bit & 1:
                at = at + (1 << bit) * (1 - 2 * (s // (1 << bit) % 2))
        return at

    loads = [
        pltpu.make_async_copy(up_hbm, up_v, local_sem.at[0]),
        pltpu.make_async_copy(down_hbm, down_v, local_sem.at[1]),
        pltpu.make_async_copy(x_hbm, x_v, local_sem.at[2]),
        pltpu.make_async_copy(g_hbm, gath.at[t], local_sem.at[3]),
    ]
    for cp in loads:
        cp.start()
    quarters = []
    for d in list(range(1, chips)) + [0]:
        quarters += [(d, 0), (d, 1)]

    def q_index(d, same):
        return tp_of(d, core if same else 1 - core)

    w_loads = []
    for n, (d, same) in enumerate(quarters):
        q = q_index(d, same)
        cp = pltpu.make_async_copy(
            w_hbm.at[:, pl.ds(pl.multiple_of(q * width, width), width)], w_v.at[q], local_sem.at[4 + n]
        )
        cp.start()
        w_loads.append(cp)

    moments = [
        pltpu.make_async_copy(mom_down, mom_down_v, own_sem.at[2]),
        pltpu.make_async_copy(mom_up, mom_v, own_sem.at[3]),
    ]

    barrier = pltpu.get_barrier_semaphore()
    for k in range(1, seq_count):
        pl.semaphore_signal(barrier, inc=1, device_id={"seq": peer(k)}, device_id_type=MESH)
    for d in range(1, chips):
        pl.semaphore_signal(barrier, inc=1, device_id={"tp": tp_of(d, core)}, device_id_type=MESH)
    pl.semaphore_signal(barrier, inc=1, device_id=sib, device_id_type=MESH)
    pl.semaphore_wait(barrier, seq_count - 1 + chips)

    def rows_of(c):
        return pl.ds(c * step, step)

    def ag(kind, d, c):
        if kind == "sib":
            src, slot, index, to = g_hbm.at[rows_of(c)], t, 0, sib
        elif kind == "chip":
            src, slot, index, to = g_hbm.at[rows_of(c)], t, d, {"tp": tp_of(d, core)}
        else:
            slot = tp_of(chips - d, core)
            src, index, to = gath.at[slot, rows_of(c)], chips - 1 + d, sib
        return pltpu.make_async_remote_copy(
            src_ref=src, dst_ref=gath.at[slot, rows_of(c)], send_sem=ag_send.at[index, c],
            recv_sem=ag_recv.at[index, c], device_id=to, device_id_type=MESH,
        )

    for c in range(chunks):
        for d in range(1, chips):
            ag("chip", d, c).start()
        ag("sib", 0, c).start()

    def forward(c):
        for d in range(1, chips):
            ag("chip", d, c).wait_recv()
            ag("pass", d, c).start()

    def place(i, j):
        return storage_ref[tenant_ref[j, i]]

    def picked(i):
        row = jnp.int32(0)
        for j in range(slots):
            p = place(i, j)
            row = row + jnp.where(p // owned == s, p % owned, 0)
        return row

    def slot_at(owner):
        found = jnp.int32(slots)
        for j in range(slots):
            found = jnp.where(place(s, j) // owned == owner, j, found)
        return found

    def bounds():
        pairs, at = [], jnp.int32(0)
        for j in range(slots):
            pairs.append((at, at + count_ref[j, s]))
            at = at + count_ref[j, s]
        return pairs

    spans = bounds()

    def a2a(n, k, src, dst):
        return pltpu.make_async_remote_copy(
            src_ref=src.at[peer(k)], dst_ref=dst.at[s], send_sem=a2a_send.at[n, k],
            recv_sem=a2a_recv.at[n, k], device_id={"seq": peer(k)}, device_id_type=MESH,
        )

    exchanges = [(send_up, recv_up), (send_down, recv_down), (psend_down, inc_down), (psend_up, inc_up)]

    def pick_send(n, table, send, recv):
        for k in range(1, seq_count):
            j = peer(k)
            send[j] = table[picked(j)]
            a2a(n, k, send, recv).start()
        recv[s] = table[picked(s)]

    side_count = seq_count // 2
    side = s // side_count
    mirror = seq_count - wide_of
    near = range(1, side_count)
    far = range(side_count, seq_count)

    def owner_of(i, j):
        return place(i, j) // owned

    def needs(i, owner):
        hit = jnp.int32(0)
        for j in range(slots):
            hit = hit + (owner_of(i, j) == owner).astype(jnp.int32)
        return hit

    def any_gap(flags, upto):
        full = jnp.int32(0)
        for flag in flags[:upto]:
            full = full + flag
        return (full < upto).astype(jnp.int32)

    def packed_at(flags, c):
        before = jnp.int32(0)
        for n, flag in enumerate(flags):
            before = before + jnp.where(n < c, flag, 0)
        return jnp.clip(c - (before < c).astype(jnp.int32), 0, slots - 2)

    if relayed:
        via, cand, mid_send, parts_send, parts_held, owner_send, cand_send, cand_recv, mid_sem, mid_recv, parts_sem, parts_recv, owner_sem = relay_refs

        def mirrored(k):
            return peer(k ^ mirror)

        def to_relay(k):
            return pltpu.make_async_remote_copy(
                src_ref=via.at[k], dst_ref=cand.at[s % side_count], send_sem=cand_send.at[k], recv_sem=cand_recv.at[k],
                device_id={"seq": peer(k)}, device_id_type=MESH,
            )

        def across(j):
            return pltpu.make_async_remote_copy(
                src_ref=mid_send.at[j], dst_ref=recv_down.at[seq_count + j], send_sem=mid_sem.at[j],
                recv_sem=mid_recv.at[j], device_id={"seq": peer(mirror)}, device_id_type=MESH,
            )

        def relay_maps():
            for k in near:
                to_relay(k).wait_recv()
            flags = [needs(peer(mirror), side * side_count + c) for c in range(side_count)]
            for j in range(slots - 1):
                mid_send[j] = cand[j + any_gap(flags, j + 1)]
                across(j).start()

        def parts_copy(j):
            return pltpu.make_async_remote_copy(
                src_ref=parts_send.at[j], dst_ref=parts_held.at[j], send_sem=parts_sem.at[j],
                recv_sem=parts_recv.at[j], device_id={"seq": peer(mirror)}, device_id_type=MESH,
            )

        def owner_copy(k):
            return pltpu.make_async_remote_copy(
                src_ref=owner_send.at[k], dst_ref=inc_down.at[peer(mirror)], send_sem=owner_sem.at[k],
                recv_sem=a2a_recv.at[2, k ^ mirror], device_id={"seq": peer(k)}, device_id_type=MESH,
            )

        def relay_parts():
            for j in range(slots - 1):
                parts_copy(j).wait_recv()
            source = peer(mirror)
            flags = [(owner_of(source, j) // side_count == side).astype(jnp.int32) for j in range(slots)]

            def term(o):
                slot = jnp.int32(0)
                for j in range(slots):
                    slot = slot + jnp.where(owner_of(source, j) == o, j, 0)
                return parts_held[packed_at(flags, slot)]

            for k in near:
                owner_send[k] = term(peer(k))
                owner_copy(k).start()
            inc_down[source] = term(s)

    if relayed:
        loads[1].wait()
        for k in near:
            via[k] = down_v[picked(mirrored(k))]
            to_relay(k).start()
        cand[s % side_count] = down_v[picked(peer(mirror))]

        loads[0].wait()
        pick_send(0, up_v, send_up, recv_up)
        for k in near:
            send_down[peer(k)] = down_v[picked(peer(k))]
            a2a(1, k, send_down, recv_down).start()
        recv_down[s] = down_v[picked(s)]
    else:
        loads[0].wait()
        pick_send(0, up_v, send_up, recv_up)
        loads[1].wait()
        pick_send(1, down_v, send_down, recv_down)

    for cp in moments:
        cp.start()

    def sib_copy(d):
        q = q_index(d, 0)
        return pltpu.make_async_remote_copy(
            src_ref=mine.at[q], dst_ref=psib.at[lax.rem(chip + d, chips)], send_sem=sib_send.at[d],
            recv_sem=sib_recv.at[d], device_id=sib, device_id_type=MESH,
        )

    loads[2].wait()
    for n, (d, same) in enumerate(quarters):
        q = q_index(d, same)
        w_loads[n].wait()

        @pl.loop(0, width // tile)
        def _(j):
            cols = pl.ds(pl.multiple_of(j * tile, tile), tile)
            mine[q, :, cols] = matmul(x_v[...], w_v[q, :, cols]).astype(jnp.bfloat16)

        if not same:
            sib_copy(d).start()

    def back_term(slot, first=False):
        @pl.loop(0, width // tile)
        def _(j):
            cols = pl.ds(pl.multiple_of(j * tile, tile), tile)
            term = matmul(gath[slot], w_v[slot, cols, :], contract_last)
            if first:
                acc[:, cols] = term
            else:
                acc[:, cols] = acc[:, cols] + term

    loads[3].wait()
    forward(0)
    back_term(t, True)
    early = max(1, chunks // 2)
    for c in range(1, early - 1):
        forward(c)
    for c in range(chunks):
        ag("sib", 0, c).wait_recv()
    if relayed:
        relay_maps()
    back_term(sib["tp"])
    for c in range(max(1, early - 1), early):
        forward(c)

    def sx(d, c):
        return pltpu.make_async_remote_copy(
            src_ref=mine.at[tp_of(d, core), rows_of(c)], dst_ref=srecv.at[chip, rows_of(c)], send_sem=sx_send.at[d, c],
            recv_sem=sx_recv.at[d, c], device_id={"tp": tp_of(d, core)}, device_id_type=MESH,
        )

    for d in range(1, chips):
        q = tp_of(d, core)
        sib_copy(d).wait_recv()
        for c in range(chunks):
            @pl.loop(0, step // part_rows)
            def _(j):
                rows = pl.ds(pl.multiple_of(c * step + j * part_rows, part_rows), part_rows)
                both = mine[q, rows, :].astype(jnp.float32) + psib[lax.rem(chip + d, chips), rows, :].astype(jnp.float32)
                mine[q, rows, :] = both.astype(jnp.bfloat16)


    def send_sums(begin, end):
        for c in range(begin, end):
            for d in range(1, chips):
                sx(d, c).start()

    block = next(n for n in (192, 128, 64, 16) if half % n == 0)
    lane = lax.broadcasted_iota(jnp.int32, (block, pair), 1)
    row_iota = lax.broadcasted_iota(jnp.int32, (block, pair), 0)

    def member(group, first_row):
        lo = jnp.where(lane < rank, spans[2 * group][0], spans[2 * group + 1][0]) - first_row
        hi = jnp.where(lane < rank, spans[2 * group][1], spans[2 * group + 1][1]) - first_row
        return (row_iota >= lo) & (row_iota < hi)

    def gather_slots(recv, slot_v, apart=False):
        for j in range(slots):
            at = owner_of(s, j)
            if apart:
                flags = [needs(s, (1 - side) * side_count + c) for c in range(side_count)]
                at = jnp.where(at // side_count == side, at, seq_count + packed_at(flags, at % side_count))
            slot_v[j * rank:(j + 1) * rank] = recv[at]

    def project(n, rows_at, slot_v):
        @pl.loop(0, half // block)
        def _(j):
            both = []
            for side in range(2):
                first_row = j * block + side * half
                product = matmul(rows_at(first_row), slot_v[...], contract_last)
                total = jnp.zeros((block, pair), jnp.float32)
                for group in range(slots // 2):
                    total = total + jnp.where(member(group, first_row), product[:, group * pair:(group + 1) * pair], 0.0)
                both.append(total + pltpu.roll(total, rank, 1))
            packed[n, pl.ds(pl.multiple_of(j * block, block), block)] = jnp.where(lane < rank, both[0], both[1]).astype(jnp.bfloat16)

    def rank_copy(n, kind, d=0):
        if kind == "half":
            src, dst, index, to = packed.at[n, pl.ds(pl.multiple_of((1 - core) * quarter, quarter), quarter)], half_recv.at[n], 0, sib
        elif kind == "chip":
            src, dst, index, to = half_sum.at[n], sum_recv.at[n, chip], d, {"tp": tp_of(d, core)}
        else:
            at = pl.ds(pl.multiple_of(core * quarter, quarter), quarter)
            src, dst, index, to = low_all.at[n, at], low_all.at[n, at], chips, sib
        return pltpu.make_async_remote_copy(
            src_ref=src, dst_ref=dst, send_sem=rank_send.at[n, index], recv_sem=rank_recv.at[n, index],
            device_id=to, device_id_type=MESH,
        )

    def reduce_first(n):
        rank_copy(n, "half").start()
        rank_copy(n, "half").wait_recv()
        own = packed[n, pl.ds(pl.multiple_of(core * quarter, quarter), quarter)].astype(jnp.float32)
        half_sum[n] = (own + half_recv[n].astype(jnp.float32)).astype(jnp.bfloat16)
        for d in range(1, chips):
            rank_copy(n, "chip", d).start()

    def reduce_last(n, scale):
        total = half_sum[n].astype(jnp.float32)
        for d in range(1, chips):
            rank_copy(n, "chip", d).wait_recv()
            total = total + sum_recv[n, lax.rem(chip + chips - d, chips)].astype(jnp.float32)
        low_all[n, pl.ds(pl.multiple_of(core * quarter, quarter), quarter)] = (scale * total).astype(jnp.bfloat16)
        rank_copy(n, "whole").start()
        rank_copy(n, "whole").wait_recv()

    def spread(n, j, side):
        values = low_all[n, pl.ds(pl.multiple_of(j * block, block), block)].astype(jnp.float32)
        turned = pltpu.roll(values, rank, 1)
        wide = jnp.where((lane < rank) == (side == 0), values, turned)
        first_row = j * block + side * half
        return jnp.concatenate(
            [jnp.where(member(group, first_row), wide, 0.0).astype(jnp.bfloat16) for group in range(slots // 2)], axis=1
        )

    def spread_into(n, wide_v):
        for side in range(2):
            @pl.loop(0, half // block)
            def _(j):
                wide_v[pl.ds(pl.multiple_of(side * half + j * block, block), block)] = spread(n, j, side)

    part[slots] = jnp.zeros((rank, width), jnp.bfloat16)

    def return_parts(n, wide_v, rows, scale, psend, incoming):
        @pl.loop(0, width // tile)
        def _(j):
            cols = pl.ds(pl.multiple_of(j * tile, tile), tile)
            term = (scale * matmul(wide_v[...], rows[:, cols], contract_leading)).astype(jnp.bfloat16)
            for k in range(slots):
                part[k, :, cols] = term[k * rank:(k + 1) * rank]

        if relayed and n == 2:
            flags = [(owner_of(s, j) // side_count != side).astype(jnp.int32) for j in range(slots)]
            for j in range(slots - 1):
                parts_send[j] = part[j + any_gap(flags, j + 1)]
                parts_copy(j).start()
        for k in near if relayed else range(1, seq_count):
            j = peer(k)
            psend[j] = part[slot_at(j)]
            a2a(n, k, psend, incoming).start()
        if relayed and n == 3:
            relay_parts()
            for k in far:
                j = peer(k)
                psend[j] = part[slot_at(j)]
                a2a(n, k, psend, incoming).start()
        psend[s] = part[slot_at(s)]
        pltpu.make_async_copy(psend.at[s], incoming.at[s], own_sem.at[n - 2]).start()

    def take_parts(n):
        src, dst = exchanges[n]
        pltpu.make_async_copy(src.at[s], dst.at[s], own_sem.at[n - 2]).wait()
        for k in range(1, seq_count):
            if not (relayed and n == 2 and k == mirror):
                a2a(n, k, src, dst).wait_recv()

    def run(wide_grad, wide_low):
        def finish_in():
            @pl.loop(0, width // tile)
            def _(j):
                cols = pl.ds(pl.multiple_of(j * tile, tile), tile)
                in_v[:, cols] = (acc[:, cols] + matmul(wide_grad[...], slot_down[:, cols])).astype(jnp.bfloat16)

        for k in range(1, seq_count):
            a2a(0, k, send_up, recv_up).wait_recv()
        gather_slots(recv_up, slot_up)
        project(0, lambda at: gath[t, pl.ds(pl.multiple_of(at, block), block)], slot_up)
        reduce_first(0)
        send_sums(0, min(3, chunks))
        for c in range(early, chunks):
            forward(c)
        reduce_last(0, adapter_scale)
        spread_into(0, wide_grad)
        return_parts(2, wide_grad, x_v, 1.0, psend_down, inc_down)

        for d in range(1, chips):
            back_term(tp_of(chips - d, core))
        for d in range(1, chips):
            for c in range(chunks):
                ag("pass", d, c).wait_recv()
            back_term(tp_of(chips - d, 1 - core))

        for k in near if relayed else range(1, seq_count):
            a2a(1, k, send_down, recv_down).wait_recv()
        if relayed:
            for j in range(slots - 1):
                across(j).wait_recv()
        gather_slots(recv_down, slot_down, relayed)
        project(1, lambda at: x_v[pl.ds(pl.multiple_of(at, block), block)], slot_down)
        reduce_first(1)
        send_sums(min(3, chunks), chunks)
        finish_in()
        reduce_last(1, 1.0)
        spread_into(1, wide_low)
        return_parts(3, wide_low, gath.at[t], adapter_scale, psend_up, inc_up)

        sib_copy(0).wait_recv()

        @pl.loop(0, width // tile)
        def _(j):
            cols = pl.ds(pl.multiple_of(j * tile, tile), tile)
            base = mine[t, :, cols].astype(jnp.float32) + psib[chip, :, cols].astype(jnp.float32)
            acc[:, cols] = base + adapter_scale * matmul(wide_low[...], slot_up[:, cols])

        for c in range(chunks):
            for d in range(1, chips):
                sx(d, c).wait_recv()

            @pl.loop(0, step // part_rows)
            def _(j):
                rows = pl.ds(pl.multiple_of(c * step + j * part_rows, part_rows), part_rows)
                total = acc[rows, :]
                for d in range(1, chips):
                    total = total + srecv[lax.rem(chip + chips - d, chips), rows, :].astype(jnp.float32)
                out_v[rows, :] = total.astype(jnp.bfloat16)

        for cp in moments:
            cp.wait()
        take_parts(2)
        for k in range(owned):
            tokens[k] = 0

        @pl.loop(0, seq_count)
        def _(i):
            row, uses = jnp.int32(0), jnp.int32(0)
            for j in range(slots):
                p = place(i, j)
                here = (p // owned == s).astype(jnp.int32)
                row = row + here * (p % owned)
                uses = uses + here
                for k in range(owned):
                    tokens[k] = tokens[k] + jnp.where(p == s * owned + k, count_ref[j, i], 0)
            row_at[i] = jnp.where(uses > 0, row, -1)

        @pl.loop(0, width // tile)
        def _(j):
            cols = pl.ds(pl.multiple_of(j * tile, tile), tile)
            for k in range(owned):
                def add(i, total):
                    return total + jnp.where(row_at[i] == k, inc_down[i, :, cols].astype(jnp.float32), 0.0)

                total = lax.fori_loop(0, seq_count, add, jnp.zeros((rank, tile), jnp.float32))
                step_down[k, :, cols], new_down[k, :, cols] = lion(total, tokens[k], mom_down_v[k, :, cols])

    pl.run_scoped(
        run,
        pltpu.VMEM((row_count, slots * rank), jnp.bfloat16),
        pltpu.VMEM((row_count, slots * rank), jnp.bfloat16),
    )

    for c in range(chunks):
        ag("sib", 0, c).wait_send()
        for d in range(1, chips):
            ag("chip", d, c).wait_send()
            ag("pass", d, c).wait_send()
            sx(d, c).wait_send()
    for d in range(chips):
        sib_copy(d).wait_send()
    for n in range(2):
        rank_copy(n, "half").wait_send()
        rank_copy(n, "whole").wait_send()
        for d in range(1, chips):
            rank_copy(n, "chip", d).wait_send()
    for n, (src, dst) in enumerate(exchanges):
        for k in range(1, seq_count):
            if not (relayed and n in (1, 2) and k in far):
                a2a(n, k, src, dst).wait_send()
    if relayed:
        for j in range(slots - 1):
            parts_copy(j).wait_send()
            across(j).wait_send()
        for k in near:
            to_relay(k).wait_send()
            owner_copy(k).wait_send()
    take_parts(3)


def adapter_step(storage, tenants, counts, x, g, w, down, up, mom_down, mom_up, seq_count, tp_count, relayed):
    row_count, width = x.shape
    owned, rank, _ = down.shape
    slots = tenants.shape[0]
    chips = tp_count // cores
    chunks = next(n for n in (6, 3, 2, 1) if row_count % (16 * n) == 0)
    bf16, f32 = jnp.bfloat16, jnp.float32
    dma = pltpu.SemaphoreType.DMA
    smem = pl.BlockSpec(memory_space=pltpu.SMEM)
    hbm = pl.BlockSpec(memory_space=pl.ANY)
    blocks = (seq_count, rank, width)
    vmem = lambda shape, dtype=bf16: pltpu.VMEM(shape, dtype)
    half = row_count // 2
    few = slots - 1
    sides = (seq_count // 2, rank, width)
    relay_scratch = [
        vmem(sides), vmem(sides), vmem((few, rank, width)), vmem((few, rank, width)), vmem((few, rank, width)), vmem(sides),
        dma((seq_count // 2,)), dma((seq_count // 2,)), dma((few,)), dma((few,)), dma((few,)), dma((few,)), dma((seq_count // 2,)),
    ]
    return pl.pallas_call(
        functools.partial(step_kernel, relayed, seq_count, tp_count, chunks),
        out_shape=(
            vmem((row_count, width)),
            vmem((row_count, width)),
            vmem(blocks),
            vmem((owned, rank, width), f32),
            vmem((owned, rank, width), f32),
            vmem((owned, rank, width), f32),
        ),
        in_specs=[smem] * 3 + [hbm] * 7,
        out_specs=(pl.BlockSpec(memory_space=pltpu.VMEM),) * 6,
        scratch_shapes=[
            vmem((row_count, width)),
            vmem((tp_count, width, width)),
            vmem((tp_count, row_count, width)),
            vmem((owned, rank, width)),
            vmem((owned, rank, width)),
            vmem(blocks), vmem(blocks), vmem((seq_count + slots - 1, rank, width)), vmem(blocks),
            vmem((slots * rank, width)),
            vmem((slots * rank, width)),
            vmem((slots + 1, rank, width)),
            vmem(blocks), vmem(blocks), vmem(blocks),
            vmem((tp_count, row_count, width)),
            vmem((chips, row_count, width)),
            vmem((chips, row_count, width)),
            vmem((row_count, width), f32),
            vmem((owned, rank, width), f32),
            vmem((2, half, 2 * rank)),
            vmem((2, half // 2, 2 * rank)),
            vmem((2, half // 2, 2 * rank)),
            vmem((2, chips, half // 2, 2 * rank)),
            vmem((2, half, 2 * rank)),
            dma((4 + tp_count,)),
            dma((2 * chips - 1, chunks)), dma((2 * chips - 1, chunks)),
            dma((4, seq_count)), dma((4, seq_count)),
            dma((chips,)), dma((chips,)),
            dma((chips, chunks)), dma((chips, chunks)),
            dma((2, chips + 1)), dma((2, chips + 1)),
            dma((4,)),
            pltpu.SMEM((seq_count,), jnp.int32),
            pltpu.SMEM((owned,), jnp.int32),
        ] + (relay_scratch if relayed else []),
        compiler_params=pltpu.CompilerParams(
            collective_id=1 if relayed else 0, has_side_effects=True, vmem_limit_bytes=52 * 1024 * 1024
        ),
        name="adapter_step_packed" if relayed else "adapter_step",
    )(storage, tenants, counts, x, g, w, down, up, mom_down, mom_up)


def most_kernel(side_rows, storage_ref, tenant_ref, out_ref):
    slots, seq_count = tenant_ref.shape
    most = jnp.int32(0)
    for i in range(seq_count):
        across = jnp.int32(0)
        for j in range(slots):
            high = storage_ref[tenant_ref[j, i]] >= side_rows
            across = across + (high != (i >= seq_count // 2)).astype(jnp.int32)
        most = jnp.maximum(most, across)
    out_ref[0] = most


def most_across(storage, tenants, owned):
    smem = pl.BlockSpec(memory_space=pltpu.SMEM)
    return pl.pallas_call(
        functools.partial(most_kernel, owned * (tenants.shape[1] // 2)),
        out_shape=jax.ShapeDtypeStruct((1,), jnp.int32),
        in_specs=[smem, smem],
        out_specs=smem,
        name="most_across",
    )(storage, tenants)


def finish_kernel(
    tile, storage_ref, tenant_ref, count_ref, out_v, in_v, inc_up, step_down_v, new_down_v, mom_v,
    out_hbm, in_hbm, step_down, step_up, new_down, new_up,
    step_v, new_v, total, row_at, used, tokens, store_sem, copy_sem,
):
    slots, seq_count = tenant_ref.shape
    owned, rank, width = mom_v.shape
    tiles = width // tile
    s = lax.axis_index("seq")

    def cols(j):
        return pl.ds(j * tile, tile)

    def store(j):
        return [
            pltpu.make_async_copy(step_v.at[:, :, cols(j)], step_up.at[:, :, cols(j)], store_sem.at[j, 0]),
            pltpu.make_async_copy(new_v.at[:, :, cols(j)], new_up.at[:, :, cols(j)], store_sem.at[j, 1]),
        ]

    copies = [
        pltpu.make_async_copy(src, dst, copy_sem.at[n])
        for n, (src, dst) in enumerate(((out_v, out_hbm), (in_v, in_hbm), (step_down_v, step_down), (new_down_v, new_down)))
    ]
    for cp in copies:
        cp.start()

    for k in range(owned):
        tokens[k] = 0

    @pl.loop(0, seq_count)
    def _(i):
        row = jnp.int32(0)
        uses = jnp.int32(0)
        for j in range(slots):
            p = storage_ref[tenant_ref[j, i]]
            here = (p // owned == s).astype(jnp.int32)
            row = row + here * (p % owned)
            uses = uses + here
            tokens[p % owned] = tokens[p % owned] + here * count_ref[j, i]
        row_at[i] = row
        used[i] = uses

    for j in range(tiles):
        total[...] = jnp.zeros_like(total)

        @pl.loop(0, seq_count)
        def _(i):
            @pl.when(used[i] > 0)
            def _():
                k = row_at[i]
                total[k] = total[k] + inc_up[i, :, cols(j)].astype(jnp.float32)

        @pl.loop(0, owned)
        def _(k):
            step_v[k, :, cols(j)], new_v[k, :, cols(j)] = lion(total[k], tokens[k], mom_v[k, :, cols(j)])

        for cp in store(j):
            cp.start()
    for j in range(tiles):
        for cp in store(j):
            cp.wait()
    for cp in copies:
        cp.wait()


def finish(storage, tenants, counts, out_pre, in_pre, inc_up, step_down, new_down, mom_up):
    seq_count = inc_up.shape[0]
    owned, rank, width = mom_up.shape
    tile = min(256, width)
    shape = jax.ShapeDtypeStruct(mom_up.shape, jnp.float32)
    smem = pl.BlockSpec(memory_space=pltpu.SMEM)
    hbm = pl.BlockSpec(memory_space=pl.ANY)
    state = pltpu.VMEM((owned, rank, width), jnp.float32)
    held = [
        pltpu.with_memory_space_constraint(a, pltpu.VMEM)
        for a in (out_pre, in_pre, inc_up, step_down, new_down, mom_up)
    ]
    return pl.pallas_call(
        functools.partial(finish_kernel, tile),
        out_shape=(
            jax.ShapeDtypeStruct(out_pre.shape, out_pre.dtype), jax.ShapeDtypeStruct(in_pre.shape, in_pre.dtype),
        ) + (shape,) * 4,
        in_specs=[smem] * 3 + [pl.BlockSpec(memory_space=pltpu.VMEM)] * 6,
        out_specs=(hbm,) * 6,
        scratch_shapes=[
            state, state,
            pltpu.VMEM((owned, rank, tile), jnp.float32),
            pltpu.SMEM((seq_count,), jnp.int32),
            pltpu.SMEM((seq_count,), jnp.int32),
            pltpu.SMEM((owned,), jnp.int32),
            pltpu.SemaphoreType.DMA((width // tile, 2)),
            pltpu.SemaphoreType.DMA((4,)),
        ],
        compiler_params=pltpu.CompilerParams(vmem_limit_bytes=48 * 1024 * 1024),
        name="finish",
    )(storage, tenants, counts, *held)


def local(seq_count, tp_count, x, g, w, down, up, mom_down, mom_up, storage, tenants, counts):
    tenants, counts = tenants.T, counts.T

    def steps(relayed, *operands):
        held = adapter_step(*operands, seq_count, tp_count, relayed)
        return finish(*operands[:3], *held)

    operands = (storage, tenants, counts, x, g, w, down, up, mom_down, mom_up)
    slots, owned = tenants.shape[0], down.shape[0]
    if seq_count != 8 or slots != seq_count // 2:
        return steps(False, *operands)
    return lax.cond(
        most_across(storage, tenants, owned)[0] < slots, functools.partial(steps, True), functools.partial(steps, False), *operands
    )


def solution(mesh):
    owner = P("seq", None, "tp")
    return jax.shard_map(
        functools.partial(local, mesh.shape["seq"], mesh.shape["tp"]),
        mesh=mesh,
        in_specs=(P("seq", "tp"), P("seq", "tp"), P("tp", None), owner, owner, owner, owner, P(), P(), P()),
        out_specs=(P("seq", "tp"), P("seq", "tp"), owner, owner, owner, owner),
        check_vma=False,
    )
```

```python
import functools

import jax
import jax.numpy as jnp
from jax import lax
from jax.experimental import pallas as pl
from jax.experimental.pallas import tpu as pltpu
from jax.sharding import PartitionSpec as P

adapter_scale = 2.0
beta_first = 0.9
beta_second = 0.99
soft_floor = 0.25
epsilon = 1e-06
contract_last = (((1,), (1,)), ((), ()))
contract_leading = (((0,), (0,)), ((), ()))
MESH = pl.DeviceIdType.MESH
cores = 2
wide_of = 2


def matmul(a, b, dims=(((1,), (0,)), ((), ()))):
    return lax.dot_general(a, b, dims, preferred_element_type=jnp.float32)


def lion(total, tokens, moment):
    grad = total / jnp.maximum(tokens, 1).astype(jnp.float32)
    combined = beta_first * moment + (1.0 - beta_first) * grad
    spread = jnp.sqrt(jnp.mean(combined * combined, axis=0, keepdims=True) + epsilon)
    step = combined / (jnp.abs(combined) + soft_floor * spread)
    return step, beta_second * moment + (1.0 - beta_second) * grad


def step_kernel(
    relayed, seq_count, tp_count, chunks,
    storage_ref, tenant_ref, count_ref, x_hbm, g_hbm, w_hbm, down_hbm, up_hbm, mom_down, mom_up,
    out_v, in_v, inc_up, step_down, new_down, mom_v,
    x_v, w_v, gath, down_v, up_v, send_down, send_up, recv_down, recv_up, slot_down, slot_up,
    part, inc_down, psend_down, psend_up, mine, psib, srecv, acc, mom_down_v, packed, half_recv, half_sum, sum_recv, low_all,
    local_sem, ag_send, ag_recv, a2a_send, a2a_recv, sib_send, sib_recv, sx_send, sx_recv, rank_send, rank_recv, own_sem, row_at, tokens, *relay_refs,
):
    s = lax.axis_index("seq")
    t = lax.axis_index("tp")
    chips = tp_count // cores
    chip = t // cores
    core = t % cores
    row_count, width = x_v.shape
    owned, rank, _ = down_v.shape
    slots = slot_down.shape[0] // rank
    sib = {"tp": chip * cores + 1 - core}
    half = row_count // 2
    quarter = half // 2
    step = row_count // chunks
    tile = min(256, width)
    pair = 2 * rank
    part_rows = 64 if step % 64 == 0 else 16

    def tp_of(d, c):
        return lax.rem(chip + d, chips) * cores + c

    def peer(k):
        if seq_count & (seq_count - 1):
            return lax.rem(s + k, seq_count)
        at = s
        for bit in range(seq_count.bit_length() - 1):
            if k >> bit & 1:
                at = at + (1 << bit) * (1 - 2 * (s // (1 << bit) % 2))
        return at

    loads = [
        pltpu.make_async_copy(up_hbm, up_v, local_sem.at[0]),
        pltpu.make_async_copy(down_hbm, down_v, local_sem.at[1]),
        pltpu.make_async_copy(x_hbm, x_v, local_sem.at[2]),
        pltpu.make_async_copy(g_hbm, gath.at[t], local_sem.at[3]),
    ]
    for cp in loads:
        cp.start()
    quarters = []
    for d in list(range(1, chips)) + [0]:
        quarters += [(d, 0), (d, 1)]

    def q_index(d, same):
        return tp_of(d, core if same else 1 - core)

    w_loads = []
    for n, (d, same) in enumerate(quarters):
        q = q_index(d, same)
        cp = pltpu.make_async_copy(
            w_hbm.at[:, pl.ds(pl.multiple_of(q * width, width), width)], w_v.at[q], local_sem.at[4 + n]
        )
        cp.start()
        w_loads.append(cp)

    moments = [
        pltpu.make_async_copy(mom_down, mom_down_v, own_sem.at[2]),
        pltpu.make_async_copy(mom_up, mom_v, own_sem.at[3]),
    ]

    barrier = pltpu.get_barrier_semaphore()
    for k in range(1, seq_count):
        pl.semaphore_signal(barrier, inc=1, device_id={"seq": peer(k)}, device_id_type=MESH)
    for d in range(1, chips):
        pl.semaphore_signal(barrier, inc=1, device_id={"tp": tp_of(d, core)}, device_id_type=MESH)
    pl.semaphore_signal(barrier, inc=1, device_id=sib, device_id_type=MESH)
    pl.semaphore_wait(barrier, seq_count - 1 + chips)

    def rows_of(c):
        return pl.ds(c * step, step)

    def ag(kind, d, c):
        if kind == "sib":
            src, slot, index, to = g_hbm.at[rows_of(c)], t, 0, sib
        elif kind == "chip":
            src, slot, index, to = g_hbm.at[rows_of(c)], t, d, {"tp": tp_of(d, core)}
        else:
            slot = tp_of(chips - d, core)
            src, index, to = gath.at[slot, rows_of(c)], chips - 1 + d, sib
        return pltpu.make_async_remote_copy(
            src_ref=src, dst_ref=gath.at[slot, rows_of(c)], send_sem=ag_send.at[index, c],
            recv_sem=ag_recv.at[index, c], device_id=to, device_id_type=MESH,
        )

    for c in range(chunks):
        for d in range(1, chips):
            ag("chip", d, c).start()
        ag("sib", 0, c).start()

    def forward(c):
        for d in range(1, chips):
            ag("chip", d, c).wait_recv()
            ag("pass", d, c).start()

    def place(i, j):
        return storage_ref[tenant_ref[j, i]]

    def picked(i):
        row = jnp.int32(0)
        for j in range(slots):
            p = place(i, j)
            row = row + jnp.where(p // owned == s, p % owned, 0)
        return row

    def slot_at(owner):
        found = jnp.int32(slots)
        for j in range(slots):
            found = jnp.where(place(s, j) // owned == owner, j, found)
        return found

    def bounds():
        pairs, at = [], jnp.int32(0)
        for j in range(slots):
            pairs.append((at, at + count_ref[j, s]))
            at = at + count_ref[j, s]
        return pairs

    spans = bounds()

    def a2a(n, k, src, dst):
        return pltpu.make_async_remote_copy(
            src_ref=src.at[peer(k)], dst_ref=dst.at[s], send_sem=a2a_send.at[n, k],
            recv_sem=a2a_recv.at[n, k], device_id={"seq": peer(k)}, device_id_type=MESH,
        )

    exchanges = [(send_up, recv_up), (send_down, recv_down), (psend_down, inc_down), (psend_up, inc_up)]

    def pick_send(n, table, send, recv):
        for k in range(1, seq_count):
            j = peer(k)
            send[j] = table[picked(j)]
            a2a(n, k, send, recv).start()
        recv[s] = table[picked(s)]

    side_count = seq_count // 2
    side = s // side_count
    mirror = seq_count - wide_of
    near = range(1, side_count)
    far = range(side_count, seq_count)

    def owner_of(i, j):
        return place(i, j) // owned

    def needs(i, owner):
        hit = jnp.int32(0)
        for j in range(slots):
            hit = hit + (owner_of(i, j) == owner).astype(jnp.int32)
        return hit

    def any_gap(flags, upto):
        full = jnp.int32(0)
        for flag in flags[:upto]:
            full = full + flag
        return (full < upto).astype(jnp.int32)

    def packed_at(flags, c):
        before = jnp.int32(0)
        for n, flag in enumerate(flags):
            before = before + jnp.where(n < c, flag, 0)
        return jnp.clip(c - (before < c).astype(jnp.int32), 0, slots - 2)

    if relayed:
        via, cand, mid_send, parts_send, parts_held, owner_send, cand_send, cand_recv, mid_sem, mid_recv, parts_sem, parts_recv, owner_sem = relay_refs

        def mirrored(k):
            return peer(k ^ mirror)

        def to_relay(k):
            return pltpu.make_async_remote_copy(
                src_ref=via.at[k], dst_ref=cand.at[s % side_count], send_sem=cand_send.at[k], recv_sem=cand_recv.at[k],
                device_id={"seq": peer(k)}, device_id_type=MESH,
            )

        def across(j):
            return pltpu.make_async_remote_copy(
                src_ref=mid_send.at[j], dst_ref=recv_down.at[seq_count + j], send_sem=mid_sem.at[j],
                recv_sem=mid_recv.at[j], device_id={"seq": peer(mirror)}, device_id_type=MESH,
            )

        def relay_maps():
            for k in near:
                to_relay(k).wait_recv()
            flags = [needs(peer(mirror), side * side_count + c) for c in range(side_count)]
            for j in range(slots - 1):
                mid_send[j] = cand[j + any_gap(flags, j + 1)]
                across(j).start()

        def parts_copy(j):
            return pltpu.make_async_remote_copy(
                src_ref=parts_send.at[j], dst_ref=parts_held.at[j], send_sem=parts_sem.at[j],
                recv_sem=parts_recv.at[j], device_id={"seq": peer(mirror)}, device_id_type=MESH,
            )

        def owner_copy(k):
            return pltpu.make_async_remote_copy(
                src_ref=owner_send.at[k], dst_ref=inc_down.at[peer(mirror)], send_sem=owner_sem.at[k],
                recv_sem=a2a_recv.at[2, k ^ mirror], device_id={"seq": peer(k)}, device_id_type=MESH,
            )

        def relay_parts():
            for j in range(slots - 1):
                parts_copy(j).wait_recv()
            source = peer(mirror)
            flags = [(owner_of(source, j) // side_count == side).astype(jnp.int32) for j in range(slots)]

            def term(o):
                slot = jnp.int32(0)
                for j in range(slots):
                    slot = slot + jnp.where(owner_of(source, j) == o, j, 0)
                return parts_held[packed_at(flags, slot)]

            for k in near:
                owner_send[k] = term(peer(k))
                owner_copy(k).start()
            inc_down[source] = term(s)

    if relayed:
        loads[1].wait()
        for k in near:
            via[k] = down_v[picked(mirrored(k))]
            to_relay(k).start()
        cand[s % side_count] = down_v[picked(peer(mirror))]

        loads[0].wait()
        pick_send(0, up_v, send_up, recv_up)
        for k in near:
            send_down[peer(k)] = down_v[picked(peer(k))]
            a2a(1, k, send_down, recv_down).start()
        recv_down[s] = down_v[picked(s)]
    else:
        loads[0].wait()
        pick_send(0, up_v, send_up, recv_up)
        loads[1].wait()
        pick_send(1, down_v, send_down, recv_down)

    for cp in moments:
        cp.start()

    def sib_copy(d):
        q = q_index(d, 0)
        return pltpu.make_async_remote_copy(
            src_ref=mine.at[q], dst_ref=psib.at[lax.rem(chip + d, chips)], send_sem=sib_send.at[d],
            recv_sem=sib_recv.at[d], device_id=sib, device_id_type=MESH,
        )

    loads[2].wait()
    for n, (d, same) in enumerate(quarters):
        q = q_index(d, same)
        w_loads[n].wait()

        @pl.loop(0, width // tile)
        def _(j):
            cols = pl.ds(pl.multiple_of(j * tile, tile), tile)
            mine[q, :, cols] = matmul(x_v[...], w_v[q, :, cols]).astype(jnp.bfloat16)

        if not same:
            sib_copy(d).start()

    def back_term(slot, first=False):
        @pl.loop(0, width // tile)
        def _(j):
            cols = pl.ds(pl.multiple_of(j * tile, tile), tile)
            term = matmul(gath[slot], w_v[slot, cols, :], contract_last)
            if first:
                acc[:, cols] = term
            else:
                acc[:, cols] = acc[:, cols] + term

    loads[3].wait()
    forward(0)
    back_term(t, True)
    early = max(1, chunks // 2)
    for c in range(1, early - 1):
        forward(c)
    for c in range(chunks):
        ag("sib", 0, c).wait_recv()
    if relayed:
        relay_maps()
    back_term(sib["tp"])
    for c in range(max(1, early - 1), early):
        forward(c)

    def sx(d, c):
        return pltpu.make_async_remote_copy(
            src_ref=mine.at[tp_of(d, core), rows_of(c)], dst_ref=srecv.at[chip, rows_of(c)], send_sem=sx_send.at[d, c],
            recv_sem=sx_recv.at[d, c], device_id={"tp": tp_of(d, core)}, device_id_type=MESH,
        )

    for d in range(1, chips):
        q = tp_of(d, core)
        sib_copy(d).wait_recv()
        for c in range(chunks):
            @pl.loop(0, step // part_rows)
            def _(j):
                rows = pl.ds(pl.multiple_of(c * step + j * part_rows, part_rows), part_rows)
                both = mine[q, rows, :].astype(jnp.float32) + psib[lax.rem(chip + d, chips), rows, :].astype(jnp.float32)
                mine[q, rows, :] = both.astype(jnp.bfloat16)


    def send_sums(begin, end):
        for c in range(begin, end):
            for d in range(1, chips):
                sx(d, c).start()

    block = next(n for n in (192, 128, 64, 16) if half % n == 0)
    lane = lax.broadcasted_iota(jnp.int32, (block, pair), 1)
    row_iota = lax.broadcasted_iota(jnp.int32, (block, pair), 0)

    def member(group, first_row):
        lo = jnp.where(lane < rank, spans[2 * group][0], spans[2 * group + 1][0]) - first_row
        hi = jnp.where(lane < rank, spans[2 * group][1], spans[2 * group + 1][1]) - first_row
        return (row_iota >= lo) & (row_iota < hi)

    def gather_slots(recv, slot_v, apart=False):
        for j in range(slots):
            at = owner_of(s, j)
            if apart:
                flags = [needs(s, (1 - side) * side_count + c) for c in range(side_count)]
                at = jnp.where(at // side_count == side, at, seq_count + packed_at(flags, at % side_count))
            slot_v[j * rank:(j + 1) * rank] = recv[at]

    def project(n, rows_at, slot_v):
        @pl.loop(0, half // block)
        def _(j):
            both = []
            for side in range(2):
                first_row = j * block + side * half
                product = matmul(rows_at(first_row), slot_v[...], contract_last)
                total = jnp.zeros((block, pair), jnp.float32)
                for group in range(slots // 2):
                    total = total + jnp.where(member(group, first_row), product[:, group * pair:(group + 1) * pair], 0.0)
                both.append(total + pltpu.roll(total, rank, 1))
            packed[n, pl.ds(pl.multiple_of(j * block, block), block)] = jnp.where(lane < rank, both[0], both[1]).astype(jnp.bfloat16)

    def rank_copy(n, kind, d=0):
        if kind == "half":
            src, dst, index, to = packed.at[n, pl.ds(pl.multiple_of((1 - core) * quarter, quarter), quarter)], half_recv.at[n], 0, sib
        elif kind == "chip":
            src, dst, index, to = half_sum.at[n], sum_recv.at[n, chip], d, {"tp": tp_of(d, core)}
        else:
            at = pl.ds(pl.multiple_of(core * quarter, quarter), quarter)
            src, dst, index, to = low_all.at[n, at], low_all.at[n, at], chips, sib
        return pltpu.make_async_remote_copy(
            src_ref=src, dst_ref=dst, send_sem=rank_send.at[n, index], recv_sem=rank_recv.at[n, index],
            device_id=to, device_id_type=MESH,
        )

    def reduce_first(n):
        rank_copy(n, "half").start()
        rank_copy(n, "half").wait_recv()
        own = packed[n, pl.ds(pl.multiple_of(core * quarter, quarter), quarter)].astype(jnp.float32)
        half_sum[n] = (own + half_recv[n].astype(jnp.float32)).astype(jnp.bfloat16)
        for d in range(1, chips):
            rank_copy(n, "chip", d).start()

    def reduce_last(n, scale):
        total = half_sum[n].astype(jnp.float32)
        for d in range(1, chips):
            rank_copy(n, "chip", d).wait_recv()
            total = total + sum_recv[n, lax.rem(chip + chips - d, chips)].astype(jnp.float32)
        low_all[n, pl.ds(pl.multiple_of(core * quarter, quarter), quarter)] = (scale * total).astype(jnp.bfloat16)
        rank_copy(n, "whole").start()
        rank_copy(n, "whole").wait_recv()

    def spread(n, j, side):
        values = low_all[n, pl.ds(pl.multiple_of(j * block, block), block)].astype(jnp.float32)
        turned = pltpu.roll(values, rank, 1)
        wide = jnp.where((lane < rank) == (side == 0), values, turned)
        first_row = j * block + side * half
        return jnp.concatenate(
            [jnp.where(member(group, first_row), wide, 0.0).astype(jnp.bfloat16) for group in range(slots // 2)], axis=1
        )

    def spread_into(n, wide_v):
        for side in range(2):
            @pl.loop(0, half // block)
            def _(j):
                wide_v[pl.ds(pl.multiple_of(side * half + j * block, block), block)] = spread(n, j, side)

    part[slots] = jnp.zeros((rank, width), jnp.bfloat16)

    def return_parts(n, wide_v, rows, scale, psend, incoming):
        @pl.loop(0, width // tile)
        def _(j):
            cols = pl.ds(pl.multiple_of(j * tile, tile), tile)
            term = (scale * matmul(wide_v[...], rows[:, cols], contract_leading)).astype(jnp.bfloat16)
            for k in range(slots):
                part[k, :, cols] = term[k * rank:(k + 1) * rank]

        if relayed and n == 2:
            flags = [(owner_of(s, j) // side_count != side).astype(jnp.int32) for j in range(slots)]
            for j in range(slots - 1):
                parts_send[j] = part[j + any_gap(flags, j + 1)]
                parts_copy(j).start()
        for k in near if relayed else range(1, seq_count):
            j = peer(k)
            psend[j] = part[slot_at(j)]
            a2a(n, k, psend, incoming).start()
        if relayed and n == 3:
            relay_parts()
            for k in far:
                j = peer(k)
                psend[j] = part[slot_at(j)]
                a2a(n, k, psend, incoming).start()
        psend[s] = part[slot_at(s)]
        pltpu.make_async_copy(psend.at[s], incoming.at[s], own_sem.at[n - 2]).start()

    def take_parts(n):
        src, dst = exchanges[n]
        pltpu.make_async_copy(src.at[s], dst.at[s], own_sem.at[n - 2]).wait()
        for k in range(1, seq_count):
            if not (relayed and n == 2 and k == mirror):
                a2a(n, k, src, dst).wait_recv()

    def run(wide_grad, wide_low):
        def finish_in():
            @pl.loop(0, width // tile)
            def _(j):
                cols = pl.ds(pl.multiple_of(j * tile, tile), tile)
                in_v[:, cols] = (acc[:, cols] + matmul(wide_grad[...], slot_down[:, cols])).astype(jnp.bfloat16)

        for k in range(1, seq_count):
            a2a(0, k, send_up, recv_up).wait_recv()
        gather_slots(recv_up, slot_up)
        project(0, lambda at: gath[t, pl.ds(pl.multiple_of(at, block), block)], slot_up)
        reduce_first(0)
        send_sums(0, min(3, chunks))
        for c in range(early, chunks):
            forward(c)
        reduce_last(0, adapter_scale)
        spread_into(0, wide_grad)
        return_parts(2, wide_grad, x_v, 1.0, psend_down, inc_down)

        for d in range(1, chips):
            back_term(tp_of(chips - d, core))
        for d in range(1, chips):
            for c in range(chunks):
                ag("pass", d, c).wait_recv()
            back_term(tp_of(chips - d, 1 - core))

        for k in near if relayed else range(1, seq_count):
            a2a(1, k, send_down, recv_down).wait_recv()
        if relayed:
            for j in range(slots - 1):
                across(j).wait_recv()
        gather_slots(recv_down, slot_down, relayed)
        project(1, lambda at: x_v[pl.ds(pl.multiple_of(at, block), block)], slot_down)
        reduce_first(1)
        send_sums(min(3, chunks), chunks)
        finish_in()
        reduce_last(1, 1.0)
        spread_into(1, wide_low)
        return_parts(3, wide_low, gath.at[t], adapter_scale, psend_up, inc_up)

        sib_copy(0).wait_recv()

        @pl.loop(0, width // tile)
        def _(j):
            cols = pl.ds(pl.multiple_of(j * tile, tile), tile)
            base = mine[t, :, cols].astype(jnp.float32) + psib[chip, :, cols].astype(jnp.float32)
            acc[:, cols] = base + adapter_scale * matmul(wide_low[...], slot_up[:, cols])

        for c in range(chunks):
            for d in range(1, chips):
                sx(d, c).wait_recv()

            @pl.loop(0, step // part_rows)
            def _(j):
                rows = pl.ds(pl.multiple_of(c * step + j * part_rows, part_rows), part_rows)
                total = acc[rows, :]
                for d in range(1, chips):
                    total = total + srecv[lax.rem(chip + chips - d, chips), rows, :].astype(jnp.float32)
                out_v[rows, :] = total.astype(jnp.bfloat16)

        for cp in moments:
            cp.wait()
        take_parts(2)
        for k in range(owned):
            tokens[k] = 0

        @pl.loop(0, seq_count)
        def _(i):
            row, uses = jnp.int32(0), jnp.int32(0)
            for j in range(slots):
                p = place(i, j)
                here = (p // owned == s).astype(jnp.int32)
                row = row + here * (p % owned)
                uses = uses + here
                for k in range(owned):
                    tokens[k] = tokens[k] + jnp.where(p == s * owned + k, count_ref[j, i], 0)
            row_at[i] = jnp.where(uses > 0, row, -1)

        @pl.loop(0, width // tile)
        def _(j):
            cols = pl.ds(pl.multiple_of(j * tile, tile), tile)
            for k in range(owned):
                def add(i, total):
                    return total + jnp.where(row_at[i] == k, inc_down[i, :, cols].astype(jnp.float32), 0.0)

                total = lax.fori_loop(0, seq_count, add, jnp.zeros((rank, tile), jnp.float32))
                step_down[k, :, cols], new_down[k, :, cols] = lion(total, tokens[k], mom_down_v[k, :, cols])

    pl.run_scoped(
        run,
        pltpu.VMEM((row_count, slots * rank), jnp.bfloat16),
        pltpu.VMEM((row_count, slots * rank), jnp.bfloat16),
    )

    for c in range(chunks):
        ag("sib", 0, c).wait_send()
        for d in range(1, chips):
            ag("chip", d, c).wait_send()
            ag("pass", d, c).wait_send()
            sx(d, c).wait_send()
    for d in range(chips):
        sib_copy(d).wait_send()
    for n in range(2):
        rank_copy(n, "half").wait_send()
        rank_copy(n, "whole").wait_send()
        for d in range(1, chips):
            rank_copy(n, "chip", d).wait_send()
    for n, (src, dst) in enumerate(exchanges):
        for k in range(1, seq_count):
            if not (relayed and n in (1, 2) and k in far):
                a2a(n, k, src, dst).wait_send()
    if relayed:
        for j in range(slots - 1):
            parts_copy(j).wait_send()
            across(j).wait_send()
        for k in near:
            to_relay(k).wait_send()
            owner_copy(k).wait_send()
    take_parts(3)


def adapter_step(storage, tenants, counts, x, g, w, down, up, mom_down, mom_up, seq_count, tp_count, relayed):
    row_count, width = x.shape
    owned, rank, _ = down.shape
    slots = tenants.shape[0]
    chips = tp_count // cores
    chunks = next(n for n in (6, 3, 2, 1) if row_count % (16 * n) == 0)
    bf16, f32 = jnp.bfloat16, jnp.float32
    dma = pltpu.SemaphoreType.DMA
    smem = pl.BlockSpec(memory_space=pltpu.SMEM)
    hbm = pl.BlockSpec(memory_space=pl.ANY)
    blocks = (seq_count, rank, width)
    vmem = lambda shape, dtype=bf16: pltpu.VMEM(shape, dtype)
    half = row_count // 2
    few = slots - 1
    sides = (seq_count // 2, rank, width)
    relay_scratch = [
        vmem(sides), vmem(sides), vmem((few, rank, width)), vmem((few, rank, width)), vmem((few, rank, width)), vmem(sides),
        dma((seq_count // 2,)), dma((seq_count // 2,)), dma((few,)), dma((few,)), dma((few,)), dma((few,)), dma((seq_count // 2,)),
    ]
    return pl.pallas_call(
        functools.partial(step_kernel, relayed, seq_count, tp_count, chunks),
        out_shape=(
            vmem((row_count, width)),
            vmem((row_count, width)),
            vmem(blocks),
            vmem((owned, rank, width), f32),
            vmem((owned, rank, width), f32),
            vmem((owned, rank, width), f32),
        ),
        in_specs=[smem] * 3 + [hbm] * 7,
        out_specs=(pl.BlockSpec(memory_space=pltpu.VMEM),) * 6,
        scratch_shapes=[
            vmem((row_count, width)),
            vmem((tp_count, width, width)),
            vmem((tp_count, row_count, width)),
            vmem((owned, rank, width)),
            vmem((owned, rank, width)),
            vmem(blocks), vmem(blocks), vmem((seq_count + slots - 1, rank, width)), vmem(blocks),
            vmem((slots * rank, width)),
            vmem((slots * rank, width)),
            vmem((slots + 1, rank, width)),
            vmem(blocks), vmem(blocks), vmem(blocks),
            vmem((tp_count, row_count, width)),
            vmem((chips, row_count, width)),
            vmem((chips, row_count, width)),
            vmem((row_count, width), f32),
            vmem((owned, rank, width), f32),
            vmem((2, half, 2 * rank)),
            vmem((2, half // 2, 2 * rank)),
            vmem((2, half // 2, 2 * rank)),
            vmem((2, chips, half // 2, 2 * rank)),
            vmem((2, half, 2 * rank)),
            dma((4 + tp_count,)),
            dma((2 * chips - 1, chunks)), dma((2 * chips - 1, chunks)),
            dma((4, seq_count)), dma((4, seq_count)),
            dma((chips,)), dma((chips,)),
            dma((chips, chunks)), dma((chips, chunks)),
            dma((2, chips + 1)), dma((2, chips + 1)),
            dma((4,)),
            pltpu.SMEM((seq_count,), jnp.int32),
            pltpu.SMEM((owned,), jnp.int32),
        ] + (relay_scratch if relayed else []),
        compiler_params=pltpu.CompilerParams(
            collective_id=1 if relayed else 0, has_side_effects=True, vmem_limit_bytes=52 * 1024 * 1024
        ),
        name="adapter_step_packed" if relayed else "adapter_step",
    )(storage, tenants, counts, x, g, w, down, up, mom_down, mom_up)


def most_kernel(side_rows, storage_ref, tenant_ref, out_ref):
    slots, seq_count = tenant_ref.shape
    most = jnp.int32(0)
    for i in range(seq_count):
        across = jnp.int32(0)
        for j in range(slots):
            high = storage_ref[tenant_ref[j, i]] >= side_rows
            across = across + (high != (i >= seq_count // 2)).astype(jnp.int32)
        most = jnp.maximum(most, across)
    out_ref[0] = most


def most_across(storage, tenants, owned):
    smem = pl.BlockSpec(memory_space=pltpu.SMEM)
    return pl.pallas_call(
        functools.partial(most_kernel, owned * (tenants.shape[1] // 2)),
        out_shape=jax.ShapeDtypeStruct((1,), jnp.int32),
        in_specs=[smem, smem],
        out_specs=smem,
        name="most_across",
    )(storage, tenants)


def finish_kernel(
    tile, storage_ref, tenant_ref, count_ref, out_v, in_v, inc_up, step_down_v, new_down_v, mom_v,
    out_hbm, in_hbm, step_down, step_up, new_down, new_up,
    step_v, new_v, total, row_at, used, tokens, store_sem, copy_sem,
):
    slots, seq_count = tenant_ref.shape
    owned, rank, width = mom_v.shape
    tiles = width // tile
    s = lax.axis_index("seq")

    def cols(j):
        return pl.ds(j * tile, tile)

    def store(j):
        return [
            pltpu.make_async_copy(step_v.at[:, :, cols(j)], step_up.at[:, :, cols(j)], store_sem.at[j, 0]),
            pltpu.make_async_copy(new_v.at[:, :, cols(j)], new_up.at[:, :, cols(j)], store_sem.at[j, 1]),
        ]

    copies = [
        pltpu.make_async_copy(src, dst, copy_sem.at[n])
        for n, (src, dst) in enumerate(((out_v, out_hbm), (in_v, in_hbm), (step_down_v, step_down), (new_down_v, new_down)))
    ]
    for cp in copies:
        cp.start()

    for k in range(owned):
        tokens[k] = 0

    @pl.loop(0, seq_count)
    def _(i):
        row = jnp.int32(0)
        uses = jnp.int32(0)
        for j in range(slots):
            p = storage_ref[tenant_ref[j, i]]
            here = (p // owned == s).astype(jnp.int32)
            row = row + here * (p % owned)
            uses = uses + here
            tokens[p % owned] = tokens[p % owned] + here * count_ref[j, i]
        row_at[i] = row
        used[i] = uses

    for j in range(tiles):
        total[...] = jnp.zeros_like(total)

        @pl.loop(0, seq_count)
        def _(i):
            @pl.when(used[i] > 0)
            def _():
                k = row_at[i]
                total[k] = total[k] + inc_up[i, :, cols(j)].astype(jnp.float32)

        @pl.loop(0, owned)
        def _(k):
            step_v[k, :, cols(j)], new_v[k, :, cols(j)] = lion(total[k], tokens[k], mom_v[k, :, cols(j)])

        for cp in store(j):
            cp.start()
    for j in range(tiles):
        for cp in store(j):
            cp.wait()
    for cp in copies:
        cp.wait()


def finish(storage, tenants, counts, out_pre, in_pre, inc_up, step_down, new_down, mom_up):
    seq_count = inc_up.shape[0]
    owned, rank, width = mom_up.shape
    tile = min(512, width)
    shape = jax.ShapeDtypeStruct(mom_up.shape, jnp.float32)
    smem = pl.BlockSpec(memory_space=pltpu.SMEM)
    hbm = pl.BlockSpec(memory_space=pl.ANY)
    state = pltpu.VMEM((owned, rank, width), jnp.float32)
    held = [
        pltpu.with_memory_space_constraint(a, pltpu.VMEM)
        for a in (out_pre, in_pre, inc_up, step_down, new_down, mom_up)
    ]
    return pl.pallas_call(
        functools.partial(finish_kernel, tile),
        out_shape=(
            jax.ShapeDtypeStruct(out_pre.shape, out_pre.dtype), jax.ShapeDtypeStruct(in_pre.shape, in_pre.dtype),
        ) + (shape,) * 4,
        in_specs=[smem] * 3 + [pl.BlockSpec(memory_space=pltpu.VMEM)] * 6,
        out_specs=(hbm,) * 6,
        scratch_shapes=[
            state, state,
            pltpu.VMEM((owned, rank, tile), jnp.float32),
            pltpu.SMEM((seq_count,), jnp.int32),
            pltpu.SMEM((seq_count,), jnp.int32),
            pltpu.SMEM((owned,), jnp.int32),
            pltpu.SemaphoreType.DMA((width // tile, 2)),
            pltpu.SemaphoreType.DMA((4,)),
        ],
        compiler_params=pltpu.CompilerParams(vmem_limit_bytes=48 * 1024 * 1024),
        name="finish",
    )(storage, tenants, counts, *held)


def local(seq_count, tp_count, x, g, w, down, up, mom_down, mom_up, storage, tenants, counts):
    tenants, counts = tenants.T, counts.T

    def steps(relayed, *operands):
        held = adapter_step(*operands, seq_count, tp_count, relayed)
        return finish(*operands[:3], *held)

    operands = (storage, tenants, counts, x, g, w, down, up, mom_down, mom_up)
    slots, owned = tenants.shape[0], down.shape[0]
    if seq_count != 8 or slots != seq_count // 2:
        return steps(False, *operands)
    return lax.cond(
        most_across(storage, tenants, owned)[0] < slots, functools.partial(steps, True), functools.partial(steps, False), *operands
    )


def solution(mesh):
    owner = P("seq", None, "tp")
    return jax.shard_map(
        functools.partial(local, mesh.shape["seq"], mesh.shape["tp"]),
        mesh=mesh,
        in_specs=(P("seq", "tp"), P("seq", "tp"), P("tp", None), owner, owner, owner, owner, P(), P(), P()),
        out_specs=(P("seq", "tp"), P("seq", "tp"), owner, owner, owner, owner),
        check_vma=False,
    )
```
